512 devices in a mesh: group: 64 (over x, z_hi, y), tp: 8 (over z_lo, core).
Axes of the slice: x: 4, y: 4, z: 16 (z_hi: 4, z_lo: 4; z = z_hi * 4 + z_lo), core: 2. Of those that a mesh axis runs over, the one named last changes fastest.
Arguments:
- hidden: bfloat16 [64, 128, 2048], P('group', 'tp'), may hold values from -6 to 6
- w_query: bfloat16 [2048, 1024], P(None, 'tp'), may hold values from -0.125 to 0.125
- w_key: bfloat16 [2048, 1024], P(None, 'tp'), may hold values from -0.21875 to 0.21875
- w_value: bfloat16 [2048, 1024], P(None, 'tp'), may hold values from -0.5 to 0.5
- w_out: bfloat16 [1024, 2048], P('tp'), may hold values from -0.1875 to 0.1875
- cache_keys: bfloat16 [256, 256, 1024], P(None, 'group', 'tp'), may hold values from -600 to 600
- cache_values: bfloat16 [256, 256, 1024], P(None, 'group', 'tp'), may hold values from -24 to 24
- stretch_count: int32 [64], P('group'), may hold values from 4 to 12, as said below
- stretch_ids: int32 [64, 12], P('group'), may hold values from 0 to 255
- recompute_pos: int32 [64, 128], P('group'), may hold values from 0 to 3071, as said below
Outputs:
- merged_out: bfloat16 [64, 128, 2048], P('group', 'tp')
The draws below stay inside these ranges and needn't reach their ends.
Inputs may be any that keep to these rules, and one draw needn't show every extreme that they name: `stretch_count`: some request joins exactly 12 stretches and some exactly 4. `stretch_ids`: entries from slot stretch_count of a request on are not used. `recompute_pos`: strictly increasing in each request; the first is 0 and the last is stretch_count * 256 - 1 of that request.
All inputs are finite; a program needn't handle non-finite values.
Results may differ from the reference program's by a relative error of at most 0.013.
The reference program's roundings to bfloat16 on the way count: a program that leaves them out, or rounds other values in their place, can miss the bound.
Values may be sent and summed in bfloat16 or wider, within the bound.
A program may use at most 64 MiB of HBM per device.

```python
import math
import jax
import jax.numpy as jnp
import numpy as np
from jax import lax

D = 2048
HEAD_DIM = 64
HEADS = 16
STRETCH = 256
MAXCH = 12
MINCH = 4
RECOMP = 128
REQS = 64
NCHUNK = 256


def request_counts(key):
    base_key = jax.random.fold_in(key, 11)
    raw_picks = jax.random.randint(jax.random.fold_in(base_key, 1), (REQS,), 0, 100)
    counts = MINCH + (MAXCH - MINCH + 1) * raw_picks ** 4 // 100000000
    busiest = jax.random.randint(jax.random.fold_in(base_key, 2), (), 0, REQS)
    lightest = (busiest + 1 + jax.random.randint(jax.random.fold_in(base_key, 3), (), 0, REQS - 1)) % REQS
    return counts.at[busiest].set(MAXCH).at[lightest].set(MINCH).astype(jnp.int32)


def draw_stretch_count(key, part):
    return request_counts(key)


def draw_recompute_pos(key, part):
    counts = request_counts(key)
    totals = counts * STRETCH
    index_range = jnp.arange(RECOMP, dtype=jnp.int32)
    starts = index_range[None, :] * totals[:, None] // RECOMP
    stops = (index_range[None, :] + 1) * totals[:, None] // RECOMP
    offsets = jax.random.randint(jax.random.fold_in(key, 29), (REQS, RECOMP), 0, 1 << 20) % (stops - starts)
    positions = starts + offsets
    positions = positions.at[:, 0].set(0)
    positions = positions.at[:, RECOMP - 1].set(totals - 1)
    return positions.astype(jnp.int32)


def draw_cache_keys(key, part):
    shape = (NCHUNK, STRETCH, HEADS * HEAD_DIM)
    values = jax.random.normal(jax.random.fold_in(key, 41), shape, jnp.float32) * 1.6
    return jnp.clip(values, -9.6, 9.6).astype(jnp.bfloat16)


def plant(values, key, least, high):
    spot = [jax.random.randint(jax.random.fold_in(key, axis), (), 0, length) for axis, length in enumerate(values.shape)]
    longest = values.shape.index(max(values.shape))
    neighbour = spot[:longest] + [(spot[longest] + 1) % values.shape[longest]] + spot[longest + 1:]
    return values.at[tuple(spot)].set(least).at[tuple(neighbour)].set(high)


def level_of(rng, shape, split, least, high):
    loudness, own = 1.0, jax.random.fold_in(rng, 6)
    for dim, shards_of in split:
        heights = jnp.exp(jax.random.uniform(jax.random.fold_in(own, dim), (shards_of,), jnp.float32, least / len(split), high / len(split)))
        loudness = loudness * jnp.repeat(heights, shape[dim] // shards_of).reshape([-1 if axis == dim else 1 for axis in range(len(shape))])
    return loudness


def cumulative_ranks(number_of, lean):
    loads = [(1 << 20) // math.isqrt(standing ** lean) + 1 for standing in range(1, number_of + 1)]
    deviation = 1 + sum(loads) // (1 << 30)
    return np.cumsum(np.array([max(1, weight // deviation) for weight in loads]))


def ranked_ids(stream_key, dims, count, skew):
    grid = cumulative_ranks(count, skew)
    pick = jax.random.randint(jax.random.fold_in(stream_key, 1), dims, 0, int(grid[count - 1]))
    grade = jnp.searchsorted(jnp.asarray(grid, jnp.int32), pick, side="right")
    return jax.random.permutation(jax.random.fold_in(stream_key, 2), count)[grade].astype(jnp.int32)


def normal_values(rng, extent, width, bound, pieces=(), kind=jnp.bfloat16):
    result = jax.random.normal(rng, extent, jnp.float32) * width
    if len(pieces) > 0:
        result = level_of(rng, extent, pieces, -0.22, 0.18) * result
    return jnp.clip(result, min=-bound, max=bound).astype(kind)


def setup_inputs(seed: int = 0) -> dict:
    arg_keys = jax.random.split(jax.random.key(seed), 11)
    return {
        "hidden": normal_values(arg_keys[0], (REQS, RECOMP, D), 1.0, 6.0, ((0, 64), (1, 8))),
        "w_query": normal_values(arg_keys[1], (D, HEADS * HEAD_DIM), D ** -0.5, 0.125, ((1, 8),)),
        "w_key": normal_values(arg_keys[2], (D, HEADS * HEAD_DIM), (D * 25 // 64) ** -0.5, 0.21875, ((1, 8),)),
        "w_value": normal_values(arg_keys[3], (D, HEADS * HEAD_DIM), (D // 16) ** -0.5, 0.5, ((1, 8),)),
        "w_out": normal_values(arg_keys[4], (HEADS * HEAD_DIM, D), (HEADS * HEAD_DIM) ** -0.5, 0.1875, ((0, 8),)),
        "cache_keys": draw_cache_keys(jax.random.fold_in(arg_keys[10], 71), 0),
        "cache_values": normal_values(arg_keys[6], (NCHUNK, STRETCH, HEADS * HEAD_DIM), 4.0, 24.0, ((1, 64), (2, 8))),
        "stretch_count": draw_stretch_count(jax.random.fold_in(arg_keys[10], 71), 0),
        "stretch_ids": plant(ranked_ids(arg_keys[8], (REQS, MAXCH), NCHUNK, 2), jax.random.fold_in(arg_keys[8], 3), 0, NCHUNK - 1).astype(jnp.int32),
        "recompute_pos": draw_recompute_pos(jax.random.fold_in(arg_keys[10], 71), 0),
    }


ROPE_BASE = 130000.0
EPSILON = 1e-05

def rope_tables(positions, head_dim):
    half_dim = head_dim // 2
    frequency = ROPE_BASE ** (-(jnp.arange(half_dim, dtype=jnp.float32) * 2.0 / head_dim))
    angles = positions.astype(jnp.float32)[..., None] * frequency
    return (jnp.cos(angles), jnp.sin(angles))

def rotate_half(values, cosine_table, sine_table):
    half_dim = values.shape[-1] // 2
    lower_half = values[..., :half_dim]
    upper_half = values[..., half_dim:]
    return jnp.concatenate([lower_half * cosine_table - upper_half * sine_table, upper_half * cosine_table + lower_half * sine_table], axis=-1)

def reference(hidden, w_query, w_key, w_value, w_out, cache_keys, cache_values, stretch_count, stretch_ids, recompute_pos):
    score_scale = HEAD_DIM ** (-0.5)
    key_len = MAXCH * STRETCH
    offsets = jnp.arange(MAXCH, dtype=jnp.int32) * STRETCH
    offset_cos, offset_sin = rope_tables(offsets, HEAD_DIM)
    key_positions = jnp.arange(key_len, dtype=jnp.int32)

    def one_request(request_args):
        rows_in, stretch_total, stretch_list, positions = request_args
        full_rows = rows_in.astype(jnp.float32)
        normed = (full_rows * lax.rsqrt(lax.optimization_barrier(jnp.mean(full_rows * full_rows, axis=-1, keepdims=True)) + EPSILON)).astype(jnp.bfloat16)
        query_cos, query_sin = rope_tables(positions, HEAD_DIM)

        def project(weight):
            return jnp.dot(normed, weight, preferred_element_type=jnp.float32).reshape(RECOMP, HEADS, HEAD_DIM)
        queries = rotate_half(project(w_query), query_cos[:, None, :], query_sin[:, None, :]).astype(jnp.bfloat16)
        fresh_keys = rotate_half(project(w_key), query_cos[:, None, :], query_sin[:, None, :]).astype(jnp.bfloat16)
        fresh_values = project(w_value).astype(jnp.bfloat16)
        cached_keys = cache_keys[stretch_list].reshape(MAXCH, STRETCH, HEADS, HEAD_DIM).astype(jnp.float32)
        cached_keys = rotate_half(cached_keys, offset_cos[:, None, None, :], offset_sin[:, None, None, :]).astype(jnp.bfloat16)
        cached_keys = cached_keys.reshape(key_len, HEADS, HEAD_DIM)
        cached_values = cache_values[stretch_list].reshape(key_len, HEADS, HEAD_DIM)
        marked = jnp.zeros((key_len,), jnp.int32).at[positions].set(1)
        keep_mask = (marked == 0) & (key_positions < stretch_total * STRETCH)
        usable = keep_mask[None, :] & (key_positions[None, :] <= positions[:, None])
        fresh_usable = positions[None, :] <= positions[:, None]
        float_queries = queries.astype(jnp.float32)
        scores = jnp.einsum('qhd,khd->hqk', float_queries, cached_keys.astype(jnp.float32)) * score_scale
        fresh_scores = jnp.einsum('qhd,khd->hqk', float_queries, fresh_keys.astype(jnp.float32)) * score_scale
        row_max = jnp.maximum(lax.optimization_barrier(jnp.max(jnp.where(usable[None], scores, -jnp.inf), axis=-1)), lax.optimization_barrier(jnp.max(jnp.where(fresh_usable[None], fresh_scores, -jnp.inf), axis=-1)))
        weights = jnp.where(usable[None], jnp.exp(scores - row_max[..., None]), 0.0)
        fresh_weights = jnp.where(fresh_usable[None], jnp.exp(fresh_scores - row_max[..., None]), 0.0)
        denominator = lax.optimization_barrier(jnp.sum(weights, axis=-1)) + lax.optimization_barrier(jnp.sum(fresh_weights, axis=-1))
        rounded = lax.optimization_barrier(weights.astype(jnp.bfloat16))
        fresh_rounded = lax.optimization_barrier(fresh_weights.astype(jnp.bfloat16))
        numerator = jnp.einsum('hqk,khd->qhd', rounded.astype(jnp.float32), cached_values.astype(jnp.float32))
        numerator = numerator + jnp.einsum('hqk,khd->qhd', fresh_rounded.astype(jnp.float32), fresh_values.astype(jnp.float32))
        attention = (numerator / jnp.transpose(denominator)[:, :, None]).astype(jnp.bfloat16).reshape(RECOMP, HEADS * HEAD_DIM)
        return jnp.dot(attention, w_out, preferred_element_type=jnp.float32).astype(jnp.bfloat16)
    return lax.map(one_request, (hidden, stretch_count, stretch_ids, recompute_pos))
```

```python
import functools

import jax
import jax.numpy as jnp
import numpy as np
from jax import lax
from jax.experimental import pallas as pl
from jax.experimental.pallas import tpu as pltpu
from jax.sharding import PartitionSpec as P

MESH = pl.DeviceIdType.MESH
HEAD_DIM = 64
STRETCH = 256
MAXCH = 12
ROPE_BASE = 130000.0
EPSILON = 1e-05
MASKED = -1e30
FLOOR = -1e29
FAR = 1 << 20


def kernel(
    hidden,
    ids,
    count,
    pos,
    freq,
    cache_keys,
    cache_values,
    w_query,
    w_key,
    w_value,
    w_out,
    out,
    normed,
    wqkv,
    wo,
    cache32,
    ids_v,
    ids_s,
    posz,
    kv_send,
    kv,
    qx,
    fresh,
    key_cos,
    key_sin,
    key_pos,
    o_send,
    o_recv,
    st_send,
    st_recv,
    att,
    att_recv,
    part,
    part_send,
    part_recv,
    sem_load,
    sem_idz_s,
    sem_idz_r,
    sem_idp_s,
    sem_idp_r,
    sem_smem,
    sem_hid_s,
    sem_hid_r,
    sem_hidp_s,
    sem_hidp_r,
    sem_kv_s,
    sem_kv_r,
    sem_q_s,
    sem_q_r,
    sem_pos_s,
    sem_pos_r,
    sem_o_s,
    sem_o_r,
    sem_st_s,
    sem_st_r,
    sem_wo_s,
    sem_wo_r,
    sem_att_s,
    sem_att_r,
    sem_part_s,
    sem_part_r,
):
    f32, bf16 = jnp.float32, jnp.bfloat16
    g, t = lax.axis_index("group"), lax.axis_index("tp")
    gx, gz, gy = g // 16, (g // 4) % 4, g % 4
    s = gx * 4 + gy
    zl, core = t // 2, t % 2
    other = 1 - core

    def plane_id(idx):
        return (((idx // 4) * 4 + gz) * 4 + idx % 4, t)

    def z_id(step):
        return ((gx * 4 + (gz + step) % 4) * 4 + gy, t)

    def run_id(step):
        return (g, ((zl + step) % 4) * 2 + core)

    partner_id = (g, zl * 2 + other)

    def remote(src, dst, send, recv, device):
        return pltpu.make_async_remote_copy(
            src_ref=src, dst_ref=dst, send_sem=send, recv_sem=recv, device_id=device, device_id_type=MESH
        )

    loads = [
        pltpu.make_async_copy(w_query, wqkv.at[:, 0:128], sem_load.at[0]),
        pltpu.make_async_copy(w_key, wqkv.at[:, 128:256], sem_load.at[1]),
        pltpu.make_async_copy(w_value, wqkv.at[:, 256:384], sem_load.at[2]),
        pltpu.make_async_copy(w_out, wo.at[0], sem_load.at[3]),
    ]
    for load in loads:
        load.start()

    barrier = pltpu.get_barrier_semaphore()

    def greet(device):
        pl.semaphore_signal(barrier, inc=1, device_id=device, device_id_type=MESH)

    for step in (2, 1, 3):
        greet(z_id(step))

    def greet_plane(d, carry):
        greet(plane_id((s + d) % 16))
        return carry

    lax.fori_loop(1, 16, greet_plane, 0)
    for step in (1, 2, 3):
        greet(run_id(step))
    greet(partner_id)

    lane = lax.broadcasted_iota(jnp.int32, (1, 128), 1)
    ids_v[s] = jnp.where(lane == MAXCH, count[0], 0)
    ids_v[s, :, 0:MAXCH] = ids[...]
    posz[0] = pos[...]
    rows = hidden[0].astype(f32)
    normed[t] = (rows * lax.rsqrt(jnp.mean(rows * rows, axis=-1, keepdims=True) + EPSILON)).astype(bf16)

    def widen(i, carry):
        here = pl.ds(pl.multiple_of(i * 32, 32), 32)
        cache32[here, 0:4, :] = cache_keys[here].astype(f32)
        cache32[here, 4:8, :] = cache_values[here].astype(f32)
        return carry

    lax.fori_loop(0, 8, widen, 0)

    row48 = lax.broadcasted_iota(jnp.int32, (48, 128), 0)
    slot_angle = ((row48 // 4) * STRETCH).astype(f32) * freq[...]
    key_cos[...] = jnp.cos(slot_angle)
    key_sin[...] = jnp.sin(slot_angle)
    row48 = lax.broadcasted_iota(jnp.int32, (16, 48, 128), 1)
    place = lax.broadcasted_iota(jnp.int32, (16, 48, 128), 0)
    key_pos[...] = (row48 // 4) * STRETCH + 4 * (16 * (place // 4) + 4 * gz + place % 4) + row48 % 4

    pl.semaphore_wait(barrier, 22)

    def id_z(step):
        return remote(ids_v.at[s], ids_v.at[(4 - step) * 16 + s], sem_idz_s.at[step], sem_idz_r.at[4 - step], z_id(step))

    def id_z_wait(dz):
        here = ids_v.at[dz * 16 + s]
        remote(here, here, sem_idz_s.at[dz], sem_idz_r.at[dz], z_id(1)).wait_recv()

    def pos_z(step):
        return remote(posz.at[0], posz.at[4 - step], sem_pos_s.at[step], sem_pos_r.at[4 - step], z_id(step))

    def id_plane(dz, d):
        here = ids_v.at[dz * 16 + s]
        return remote(here, here, sem_idp_s.at[dz, d], sem_idp_r.at[dz, d], plane_id((s + d) % 16))

    def id_plane_wait(dz, d):
        here = ids_v.at[dz * 16 + (s + 16 - d) % 16]
        return remote(here, here, sem_idp_s.at[dz, d], sem_idp_r.at[dz, d], plane_id((s + d) % 16))

    def spread_ids(dz):
        def body(d, carry):
            id_plane(dz, d).start()
            return carry

        lax.fori_loop(1, 16, body, 0)

    for step in (2, 1, 3):
        id_z(step).start()
    spread_ids(0)
    for step in (2, 1, 3):
        pos_z(step).start()

    def hid_run(step):
        here = normed.at[t]
        return remote(here, here, sem_hid_s.at[step], sem_hid_r.at[step], run_id(step))

    def hid_run_wait(step):
        here = normed.at[((zl + 4 - step) % 4) * 2 + core]
        remote(here, here, sem_hid_s.at[step], sem_hid_r.at[step], run_id(step)).wait_recv()

    def hid_pair(step):
        here = normed.at[((zl + 4 - step) % 4) * 2 + core]
        return remote(here, here, sem_hidp_s.at[step], sem_hidp_r.at[step], partner_id)

    def hid_pair_wait(step):
        here = normed.at[((zl + 4 - step) % 4) * 2 + other]
        remote(here, here, sem_hidp_s.at[step], sem_hidp_r.at[step], partner_id).wait_recv()

    for step in (1, 2, 3):
        hid_run(step).start()
    hid_pair(0).start()
    loads[3].wait()
    wo_pair = remote(wo.at[0], wo.at[1], sem_wo_s, sem_wo_r, partner_id)
    wo_pair.start()

    low_rows = lax.broadcasted_iota(jnp.int32, (8, 128), 0) < 4

    def fill(row, target):
        for quad in range(3):
            key_rows, value_rows = [], []
            for pair in range(2):
                first = cache32[ids_s[row, 0, quad * 4 + pair * 2]]
                second = cache32[ids_s[row, 0, quad * 4 + pair * 2 + 1]]
                key_rows.append(jnp.where(low_rows, first, pltpu.roll(second, 4, 0)))
                value_rows.append(jnp.where(low_rows, pltpu.roll(first, 4, 0), second))
            target[quad * 16 : quad * 16 + 16, :] = jnp.concatenate(key_rows, 0).astype(bf16)
            target[48 + quad * 16 : 64 + quad * 16, :] = jnp.concatenate(value_rows, 0).astype(bf16)

    def kv_copy(dz, d):
        return remote(
            kv_send.at[dz, d], kv.at[dz, s], sem_kv_s.at[dz, d], sem_kv_r.at[dz, d], plane_id((s + d) % 16)
        )

    def serve(dz):
        def got(d, carry):
            id_plane_wait(dz, d).wait_recv()
            return carry

        lax.fori_loop(1, 16, got, 0)
        here = pl.ds(dz * 16, 16)
        to_smem = pltpu.make_async_copy(ids_v.at[here], ids_s.at[here], sem_smem.at[dz])
        to_smem.start()
        to_smem.wait()

        def send(d, carry):
            fill(dz * 16 + (s + d) % 16, kv_send.at[dz, d])
            kv_copy(dz, d).start()
            return carry

        lax.fori_loop(1, 16, send, 0)
        fill(dz * 16 + s, kv.at[dz, s])

    id_z_wait(1)
    spread_ids(1)
    id_z_wait(3)
    spread_ids(3)
    serve(0)
    id_z_wait(2)
    spread_ids(2)
    serve(1)
    serve(3)

    for step in (1, 2, 3):
        hid_run_wait(step)
        hid_pair(step).start()
    posf = jnp.broadcast_to(pos[...].astype(f32), (128, 128)).T
    angle = posf * freq[...]
    cos_q, sin_q = jnp.cos(angle), jnp.sin(angle)
    lanes = lax.broadcasted_iota(jnp.int32, (128, 128), 1)
    lower = lanes % 64 < 32
    for load in loads[:3]:
        load.wait()
    for step in range(4):
        hid_pair_wait(step)
    projected = jnp.dot(normed[...].reshape(128, 2048), wqkv[...], preferred_element_type=f32)

    def rotate(values):
        swapped = jnp.where(lower, -pltpu.roll(values, 96, 1), pltpu.roll(values, 32, 1))
        return (values * cos_q + swapped * sin_q).astype(bf16)

    qx[0] = (rotate(projected[:, 0:128]).astype(f32) * HEAD_DIM**-0.5).astype(bf16)
    fresh[0] = rotate(projected[:, 128:256])
    fresh[1] = projected[:, 256:384].astype(bf16)

    def q_z(step):
        return remote(qx.at[0], qx.at[4 - step], sem_q_s.at[step], sem_q_r.at[4 - step], z_id(step))

    for step in (2, 1, 3):
        q_z(step).start()
    serve(2)

    head0 = lanes < 64
    swap_row = lax.broadcasted_iota(jnp.int32, (128, 128), 0)
    swap = jnp.where(
        (lanes % 64 < 32) & (swap_row == lanes + 32),
        -1.0,
        jnp.where((lanes % 64 >= 32) & (swap_row == lanes - 32), 1.0, 0.0),
    ).astype(bf16)
    ones = jnp.ones((128, 128), bf16)
    last_dims = (((1,), (1,)), ((), ()))
    first_dims = (((0,), (0,)), ((), ()))

    def soften(keys, values, queries, usable):
        zero = jnp.zeros((), bf16)
        both = jnp.concatenate([jnp.where(head0, queries, zero), jnp.where(head0, zero, queries)], 0)
        scores = lax.dot_general(keys, both, last_dims, preferred_element_type=f32)
        tops, sums, weights = [], [], []
        for head in range(2):
            part_scores = jnp.where(usable, scores[:, head * 128 : head * 128 + 128], MASKED)
            top = jnp.maximum(jnp.max(part_scores, axis=0, keepdims=True), FLOOR)
            weight = jnp.exp(part_scores - top)
            tops.append(top)
            sums.append(jnp.sum(weight, axis=0, keepdims=True))
            weights.append(weight.astype(bf16))
        mixed = lax.dot_general(values, jnp.concatenate(weights, 1), first_dims, preferred_element_type=f32)
        return jnp.concatenate([mixed[0:64, 0:128], mixed[64:128, 128:256]], 0), tops, sums

    def attend(dz):
        def got(d, carry):
            here = kv.at[dz, (s + 16 - d) % 16]
            remote(here, here, sem_kv_s.at[dz, d], sem_kv_r.at[dz, d], plane_id((s + d) % 16)).wait_recv()
            return carry

        lax.fori_loop(1, 16, got, 0)
        raw = kv[dz, :, 0:48, :]
        turned = jnp.dot(raw.reshape(768, 128), swap, preferred_element_type=f32).reshape(16, 48, 128)
        keys = (raw.astype(f32) * key_cos[...][None] + turned * key_sin[...][None]).astype(bf16).reshape(768, 128)
        values = kv[dz, :, 48:96, :].reshape(768, 128)
        place_of = key_pos[...].reshape(768, 128)
        pos_row = posz[dz]
        pos_col = jnp.broadcast_to(pos_row, (768, 128))
        same = jnp.where(place_of == pos_col, 1.0, 0.0).astype(bf16)
        marked = jnp.dot(same, ones, preferred_element_type=f32) > 0.5
        limit = ids_s[dz * 16 + s, 0, MAXCH] * STRETCH
        usable = jnp.where(marked | (place_of >= limit), FAR, place_of) <= pos_col
        return soften(keys, values, qx[dz], usable)

    def o_copy(dz):
        return remote(o_send.at[dz], o_recv.at[4 - dz], sem_o_s.at[dz], sem_o_r.at[4 - dz], z_id(dz))

    def st_copy(dz):
        return remote(st_send.at[dz], st_recv.at[4 - dz], sem_st_s.at[dz], sem_st_r.at[4 - dz], z_id(dz))

    def wait_z(ref, send, recv, dz):
        here = ref.at[dz]
        remote(here, here, send.at[dz], recv.at[dz], z_id(1)).wait_recv()

    partials = [
        soften(fresh[0], fresh[1], qx[0], posf <= pos[...].astype(f32)),
        attend(0),
    ]
    for dz in (1, 3, 2):
        wait_z(posz, sem_pos_s, sem_pos_r, dz)
        wait_z(qx, sem_q_s, sem_q_r, dz)
        mixed, tops, sums = attend(dz)
        o_send[dz] = mixed.astype(bf16)
        st_send[dz] = jnp.concatenate(tops + sums, 0)
        o_copy(dz).start()
        st_copy(dz).start()
    for dz in (1, 3, 2):
        wait_z(o_recv, sem_o_s, sem_o_r, dz)
        wait_z(st_recv, sem_st_s, sem_st_r, dz)
        stats = st_recv[dz]
        partials.append(
            (o_recv[dz].astype(f32), [stats[0:1], stats[1:2]], [stats[2:3], stats[3:4]])
        )
    halves = []
    for head in range(2):
        top = functools.reduce(jnp.maximum, [tops[head] for _, tops, _ in partials])
        total, weight = 0.0, 0.0
        for mixed, tops, sums in partials:
            factor = jnp.exp(tops[head] - top)
            total = total + mixed[head * 64 : head * 64 + 64] * factor
            weight = weight + sums[head] * factor
        halves.append(total / weight)
    attention = jnp.concatenate(halves, 0).T.astype(bf16)
    for run in range(4):
        for half in range(2):
            att[half, run] = attention[run * 32 + half * 16 : run * 32 + half * 16 + 16]

    att_pair = remote(att.at[other], att_recv, sem_att_s, sem_att_r, partner_id)
    att_pair.start()
    wo_pair.wait_recv()
    att_pair.wait_recv()
    mine = jnp.concatenate([att[core].reshape(64, 128), att_recv[...].reshape(64, 128)], 1)
    product = jnp.dot(mine, wo[...].reshape(256, 2048), preferred_element_type=f32).reshape(4, 16, 2048)
    part[...] = product
    part_send[...] = product.astype(bf16)

    def part_copy(step):
        return remote(
            part_send.at[(zl + step) % 4], part_recv.at[step], sem_part_s.at[step], sem_part_r.at[step], run_id(step)
        )

    for step in (2, 1, 3):
        part_copy(step).start()
    summed = part[zl]
    for step in (1, 2, 3):
        part_copy(step).wait_recv()
    for step in (1, 2, 3):
        summed = summed + part_recv[step].astype(f32)
    out[0] = summed.astype(bf16)

    def drain(d, carry):
        for dz in range(4):
            id_plane(dz, d).wait_send()
            kv_copy(dz, d).wait_send()
        return carry

    lax.fori_loop(1, 16, drain, 0)
    for step in (1, 2, 3):
        id_z(step).wait_send()
        pos_z(step).wait_send()
        hid_run(step).wait_send()
        q_z(step).wait_send()
        o_copy(step).wait_send()
        st_copy(step).wait_send()
        part_copy(step).wait_send()
    for step in range(4):
        hid_pair(step).wait_send()
    wo_pair.wait_send()
    att_pair.wait_send()


def local(hidden, w_query, w_key, w_value, w_out, cache_keys, cache_values, stretch_count, stretch_ids, recompute_pos):
    half = np.arange(128) % 32
    freq = (ROPE_BASE ** (-(half * 2.0 / HEAD_DIM))).astype(np.float32)[None]
    vmem, smem, anywhere = (
        pl.BlockSpec(memory_space=pltpu.VMEM),
        pl.BlockSpec(memory_space=pltpu.SMEM),
        pl.BlockSpec(memory_space=pl.ANY),
    )
    f32, bf16, i32, dma = jnp.float32, jnp.bfloat16, jnp.int32, pltpu.SemaphoreType.DMA
    scratch = [
        pltpu.VMEM((8, 16, 2048), bf16),
        pltpu.VMEM((2048, 384), bf16),
        pltpu.VMEM((2, 128, 2048), bf16),
        pltpu.VMEM((256, 8, 128), f32),
        pltpu.VMEM((64, 1, 128), i32),
        pltpu.SMEM((64, 1, 128), i32),
        pltpu.VMEM((4, 1, 128), i32),
        pltpu.VMEM((4, 16, 96, 128), bf16),
        pltpu.VMEM((4, 16, 96, 128), bf16),
        pltpu.VMEM((4, 128, 128), bf16),
        pltpu.VMEM((2, 128, 128), bf16),
        pltpu.VMEM((48, 128), f32),
        pltpu.VMEM((48, 128), f32),
        pltpu.VMEM((16, 48, 128), i32),
        pltpu.VMEM((4, 128, 128), bf16),
        pltpu.VMEM((4, 128, 128), bf16),
        pltpu.VMEM((4, 4, 128), f32),
        pltpu.VMEM((4, 4, 128), f32),
        pltpu.VMEM((2, 4, 16, 128), bf16),
        pltpu.VMEM((4, 16, 128), bf16),
        pltpu.VMEM((4, 16, 2048), f32),
        pltpu.VMEM((4, 16, 2048), bf16),
        pltpu.VMEM((4, 16, 2048), bf16),
        dma((4,)),
        dma((4,)),
        dma((4,)),
        dma((4, 16)),
        dma((4, 16)),
        dma((4,)),
        dma((4,)),
        dma((4,)),
        dma((4,)),
        dma((4,)),
        dma((4, 16)),
        dma((4, 16)),
        dma((4,)),
        dma((4,)),
        dma((4,)),
        dma((4,)),
        dma((4,)),
        dma((4,)),
        dma((4,)),
        dma((4,)),
        dma,
        dma,
        dma,
        dma,
        dma((4,)),
        dma((4,)),
    ]
    return pl.pallas_call(
        kernel,
        out_shape=jax.ShapeDtypeStruct(hidden.shape, bf16),
        in_specs=[vmem, vmem, smem, vmem, vmem, vmem, vmem] + [anywhere] * 4,
        out_specs=vmem,
        scratch_shapes=scratch,
        compiler_params=pltpu.CompilerParams(
            collective_id=0, has_side_effects=True, vmem_limit_bytes=56 * 1024 * 1024
        ),
    )(
        hidden,
        stretch_ids,
        stretch_count,
        recompute_pos,
        jnp.asarray(freq),
        cache_keys,
        cache_values,
        w_query,
        w_key,
        w_value,
        w_out,
    )


def solution(mesh):
    placed = (
        P("group", "tp", None),
        P(None, "tp"),
        P(None, "tp"),
        P(None, "tp"),
        P("tp", None),
        P(None, "group", "tp"),
        P(None, "group", "tp"),
        P("group"),
        P("group", None),
        P("group", None),
    )
    return jax.shard_map(
        local, mesh=mesh, in_specs=placed, out_specs=P("group", "tp", None), check_vma=False
    )
```

```python
import functools

import jax
import jax.numpy as jnp
import numpy as np
from jax import lax
from jax.experimental import pallas as pl
from jax.experimental.pallas import tpu as pltpu
from jax.sharding import PartitionSpec as P

MESH = pl.DeviceIdType.MESH
HEAD_DIM = 64
STRETCH = 256
MAXCH = 12
ROPE_BASE = 130000.0
EPSILON = 1e-05
MASKED = -1e30
FLOOR = -1e29
FAR = 1 << 20
OFFSETS = (
    (0, 1), (0, 3), (1, 0), (3, 0),
    (1, 1), (1, 3), (3, 1), (3, 3), (0, 2), (2, 0),
    (1, 2), (2, 1), (3, 2), (2, 3), (2, 2),
)
STEP_X = sum(dx << (2 * i) for i, (dx, _) in enumerate(OFFSETS))
STEP_Y = sum(dy << (2 * i) for i, (_, dy) in enumerate(OFFSETS))
RINGS = ((0, 5), (5, 11), (11, 16))


def kernel(
    hidden,
    ids,
    count,
    pos,
    freq,
    cache_keys,
    cache_values,
    w_query,
    w_key,
    w_value,
    w_out,
    out,
    normed,
    wqkv,
    wo,
    cache32,
    ids_v,
    ids_s,
    posz,
    kv_send,
    kv,
    qx,
    fresh,
    key_cos,
    key_sin,
    key_pos,
    o_send,
    o_recv,
    st_send,
    st_recv,
    att,
    att_recv,
    part,
    part_send,
    part_recv,
    sem_load,
    sem_idz_s,
    sem_idz_r,
    sem_idp_s,
    sem_idp_r,
    sem_smem,
    sem_hid_s,
    sem_hid_r,
    sem_hidp_s,
    sem_hidp_r,
    sem_kv_s,
    sem_kv_r,
    sem_q_s,
    sem_q_r,
    sem_pos_s,
    sem_pos_r,
    sem_o_s,
    sem_o_r,
    sem_st_s,
    sem_st_r,
    sem_wo_s,
    sem_wo_r,
    sem_att_s,
    sem_att_r,
    sem_part_s,
    sem_part_r,
):
    f32, bf16 = jnp.float32, jnp.bfloat16
    g, t = lax.axis_index("group"), lax.axis_index("tp")
    gx, gz, gy = g // 16, (g // 4) % 4, g % 4
    s = gx * 4 + gy
    zl, core = t // 2, t % 2
    other = 1 - core

    def ahead(k):
        shift = 2 * (k - 1)
        return ((gx + (STEP_X >> shift) % 4) % 4) * 4 + (gy + (STEP_Y >> shift) % 4) % 4

    def behind(k):
        shift = 2 * (k - 1)
        return ((gx + 4 - (STEP_X >> shift) % 4) % 4) * 4 + (gy + 4 - (STEP_Y >> shift) % 4) % 4

    def plane_id(idx):
        return (((idx // 4) * 4 + gz) * 4 + idx % 4, t)

    def z_id(step):
        return ((gx * 4 + (gz + step) % 4) * 4 + gy, t)

    def run_id(step):
        return (g, ((zl + step) % 4) * 2 + core)

    partner_id = (g, zl * 2 + other)

    def remote(src, dst, send, recv, device):
        return pltpu.make_async_remote_copy(
            src_ref=src, dst_ref=dst, send_sem=send, recv_sem=recv, device_id=device, device_id_type=MESH
        )

    loads = [
        pltpu.make_async_copy(w_query, wqkv.at[:, 0:128], sem_load.at[0]),
        pltpu.make_async_copy(w_key, wqkv.at[:, 128:256], sem_load.at[1]),
        pltpu.make_async_copy(w_value, wqkv.at[:, 256:384], sem_load.at[2]),
        pltpu.make_async_copy(w_out, wo.at[0], sem_load.at[3]),
    ]
    for load in loads:
        load.start()

    barrier = pltpu.get_barrier_semaphore()

    def greet(device):
        pl.semaphore_signal(barrier, inc=1, device_id=device, device_id_type=MESH)

    for step in (1, 3):
        greet(z_id(step))

    def greet_plane(k, carry):
        greet(plane_id(ahead(k)))
        return carry

    lax.fori_loop(1, 16, greet_plane, 0)
    for step in (1, 2, 3):
        greet(run_id(step))
    greet(partner_id)

    lane = lax.broadcasted_iota(jnp.int32, (1, 128), 1)
    ids_v[0] = jnp.where(lane == MAXCH, count[0], 0)
    ids_v[0, :, 0:MAXCH] = ids[...]
    posz[0] = pos[...]
    rows = hidden[0].astype(f32)
    normed[t] = (rows * lax.rsqrt(jnp.mean(rows * rows, axis=-1, keepdims=True) + EPSILON)).astype(bf16)

    def widen(i, carry):
        here = pl.ds(pl.multiple_of(i * 32, 32), 32)
        cache32[here, 0:4, :] = cache_keys[here].astype(f32)
        cache32[here, 4:8, :] = cache_values[here].astype(f32)
        return carry

    lax.fori_loop(0, 8, widen, 0)

    row48 = lax.broadcasted_iota(jnp.int32, (48, 128), 0)
    slot_angle = ((row48 // 4) * STRETCH).astype(f32) * freq[...]
    key_cos[...] = jnp.cos(slot_angle)
    key_sin[...] = jnp.sin(slot_angle)
    row48 = lax.broadcasted_iota(jnp.int32, (16, 48, 128), 1)
    place = lax.broadcasted_iota(jnp.int32, (16, 48, 128), 0)
    key_pos[...] = (row48 // 4) * STRETCH + 4 * (16 * (place // 4) + 4 * gz + place % 4) + row48 % 4

    pl.semaphore_wait(barrier, 21)

    def id_z(step):
        return remote(ids_v.at[0], ids_v.at[(4 - step) * 16], sem_idz_s.at[step], sem_idz_r.at[4 - step], z_id(step))

    def pos_z(step):
        return remote(posz.at[0], posz.at[4 - step], sem_pos_s.at[step], sem_pos_r.at[4 - step], z_id(step))

    id_relay = remote(ids_v.at[16], ids_v.at[32], sem_idz_s.at[2], sem_idz_r.at[2], z_id(3))
    pos_relay = remote(posz.at[1], posz.at[2], sem_pos_s.at[2], sem_pos_r.at[2], z_id(3))

    def wait_z(ref, send, recv, dz):
        here = ref.at[dz]
        remote(here, here, send.at[dz], recv.at[dz], z_id(1)).wait_recv()

    def id_z_wait(dz):
        here = ids_v.at[dz * 16]
        remote(here, here, sem_idz_s.at[dz], sem_idz_r.at[dz], z_id(1)).wait_recv()

    def id_plane(dz, k):
        return remote(
            ids_v.at[dz * 16], ids_v.at[dz * 16 + k], sem_idp_s.at[dz, k], sem_idp_r.at[dz, k], plane_id(ahead(k))
        )

    def spread_ids(dz):
        def body(k, carry):
            id_plane(dz, k).start()
            return carry

        lax.fori_loop(1, 16, body, 0)

    for step in (1, 3):
        id_z(step).start()
    spread_ids(0)
    for step in (1, 3):
        pos_z(step).start()

    def hid_run(step):
        here = normed.at[t]
        return remote(here, here, sem_hid_s.at[step], sem_hid_r.at[step], run_id(step))

    def hid_run_wait(step):
        here = normed.at[((zl + 4 - step) % 4) * 2 + core]
        remote(here, here, sem_hid_s.at[step], sem_hid_r.at[step], run_id(step)).wait_recv()

    def hid_pair(step):
        here = normed.at[((zl + 4 - step) % 4) * 2 + core]
        return remote(here, here, sem_hidp_s.at[step], sem_hidp_r.at[step], partner_id)

    def hid_pair_wait(step):
        here = normed.at[((zl + 4 - step) % 4) * 2 + other]
        remote(here, here, sem_hidp_s.at[step], sem_hidp_r.at[step], partner_id).wait_recv()

    for step in (2, 1, 3):
        hid_run(step).start()
    hid_pair(0).start()
    loads[3].wait()
    wo_pair = remote(wo.at[0], wo.at[1], sem_wo_s, sem_wo_r, partner_id)
    wo_pair.start()

    low_rows = lax.broadcasted_iota(jnp.int32, (8, 128), 0) < 4

    def fill(row, target):
        for quad in range(3):
            key_rows, value_rows = [], []
            for pair in range(2):
                first = cache32[ids_s[row, 0, quad * 4 + pair * 2]]
                second = cache32[ids_s[row, 0, quad * 4 + pair * 2 + 1]]
                key_rows.append(jnp.where(low_rows, first, pltpu.roll(second, 4, 0)))
                value_rows.append(jnp.where(low_rows, pltpu.roll(first, 4, 0), second))
            target[quad * 16 : quad * 16 + 16, :] = jnp.concatenate(key_rows, 0).astype(bf16)
            target[48 + quad * 16 : 64 + quad * 16, :] = jnp.concatenate(value_rows, 0).astype(bf16)

    def kv_copy(dz, k):
        return remote(
            kv_send.at[dz, k], kv.at[dz, s], sem_kv_s.at[dz, k], sem_kv_r.at[dz, k], plane_id(behind(k))
        )

    def serve(dz, ring, backward=False):
        start, stop = ring

        def got(k, carry):
            id_plane(dz, k).wait_recv()
            return carry

        lax.fori_loop(max(start, 1), stop, got, 0)
        here = pl.ds(dz * 16 + start, stop - start)
        to_smem = pltpu.make_async_copy(ids_v.at[here], ids_s.at[here], sem_smem.at[dz, start])
        to_smem.start()
        to_smem.wait()

        def send(i, carry):
            k = stop - 1 - i if backward else max(start, 1) + i
            fill(dz * 16 + k, kv_send.at[dz, k])
            kv_copy(dz, k).start()
            return carry

        lax.fori_loop(0, stop - max(start, 1), send, 0)
        if start == 0:
            fill(dz * 16, kv.at[dz, s])

    serve(0, RINGS[0])
    serve(0, RINGS[1])
    id_z_wait(1)
    id_relay.start()
    spread_ids(1)
    id_z_wait(3)
    spread_ids(3)
    serve(0, RINGS[2])
    serve(1, RINGS[0])
    for step in (1, 2, 3):
        hid_run_wait(step)
        hid_pair(step).start()
    wait_z(posz, sem_pos_s, sem_pos_r, 1)
    pos_relay.start()
    serve(1, RINGS[1])
    id_z_wait(2)
    spread_ids(2)
    serve(1, RINGS[2])

    posf = jnp.broadcast_to(pos[...].astype(f32), (128, 128)).T
    angle = posf * freq[...]
    cos_q, sin_q = jnp.cos(angle), jnp.sin(angle)
    lanes = lax.broadcasted_iota(jnp.int32, (128, 128), 1)
    lower = lanes % 64 < 32
    for load in loads[:3]:
        load.wait()
    for step in range(4):
        hid_pair_wait(step)

    def project(first, last):
        return jnp.dot(normed[...].reshape(128, 2048), wqkv[:, first:last], preferred_element_type=f32)

    def rotate(values):
        swapped = jnp.where(lower, -pltpu.roll(values, 96, 1), pltpu.roll(values, 32, 1))
        return (values * cos_q + swapped * sin_q).astype(bf16)

    qx[0] = (rotate(project(0, 128)).astype(f32) * HEAD_DIM**-0.5).astype(bf16)

    def q_z(step):
        return remote(qx.at[0], qx.at[4 - step], sem_q_s.at[step], sem_q_r.at[4 - step], z_id(step))

    for step in (2, 1, 3):
        q_z(step).start()
    for ring in RINGS:
        serve(2, ring)
    serve(3, (0, 16), backward=True)
    projected = project(128, 384)
    fresh[0] = rotate(projected[:, 0:128])
    fresh[1] = projected[:, 128:256].astype(bf16)

    head0 = lanes < 64
    swap_row = lax.broadcasted_iota(jnp.int32, (128, 128), 0)
    swap = jnp.where(
        (lanes % 64 < 32) & (swap_row == lanes + 32),
        -1.0,
        jnp.where((lanes % 64 >= 32) & (swap_row == lanes - 32), 1.0, 0.0),
    ).astype(bf16)
    ones = jnp.ones((128, 128), bf16)
    last_dims = (((1,), (1,)), ((), ()))
    first_dims = (((0,), (0,)), ((), ()))

    def soften(keys, values, queries, usable):
        zero = jnp.zeros((), bf16)
        both = jnp.concatenate([jnp.where(head0, queries, zero), jnp.where(head0, zero, queries)], 0)
        scores = lax.dot_general(keys, both, last_dims, preferred_element_type=f32)
        tops, sums, weights = [], [], []
        for head in range(2):
            part_scores = jnp.where(usable, scores[:, head * 128 : head * 128 + 128], MASKED)
            top = jnp.maximum(jnp.max(part_scores, axis=0, keepdims=True), FLOOR)
            weight = jnp.exp(part_scores - top)
            tops.append(top)
            sums.append(jnp.sum(weight, axis=0, keepdims=True))
            weights.append(weight.astype(bf16))
        mixed = lax.dot_general(values, jnp.concatenate(weights, 1), first_dims, preferred_element_type=f32)
        return jnp.concatenate([mixed[0:64, 0:128], mixed[64:128, 128:256]], 0), tops, sums

    def attend(dz):
        def got(d, carry):
            here = kv.at[dz, ahead(d)]
            remote(here, here, sem_kv_s.at[dz, d], sem_kv_r.at[dz, d], plane_id(behind(d))).wait_recv()
            return carry

        lax.fori_loop(1, 16, got, 0)
        raw = kv[dz, :, 0:48, :]
        turned = jnp.dot(raw.reshape(768, 128), swap, preferred_element_type=f32).reshape(16, 48, 128)
        keys = (raw.astype(f32) * key_cos[...][None] + turned * key_sin[...][None]).astype(bf16).reshape(768, 128)
        values = kv[dz, :, 48:96, :].reshape(768, 128)
        place_of = key_pos[...].reshape(768, 128)
        pos_row = posz[dz]
        pos_col = jnp.broadcast_to(pos_row, (768, 128))
        same = jnp.where(place_of == pos_col, 1.0, 0.0).astype(bf16)
        marked = jnp.dot(same, ones, preferred_element_type=f32) > 0.5
        limit = ids_s[dz * 16, 0, MAXCH] * STRETCH
        usable = jnp.where(marked | (place_of >= limit), FAR, place_of) <= pos_col
        return soften(keys, values, qx[dz], usable)

    def o_copy(dz):
        return remote(o_send.at[dz], o_recv.at[4 - dz], sem_o_s.at[dz], sem_o_r.at[4 - dz], z_id(dz))

    def st_copy(dz):
        return remote(st_send.at[dz], st_recv.at[4 - dz], sem_st_s.at[dz], sem_st_r.at[4 - dz], z_id(dz))

    partials = [
        soften(fresh[0], fresh[1], qx[0], posf <= pos[...].astype(f32)),
        attend(0),
    ]
    for dz in (1, 2, 3):
        if dz > 1:
            wait_z(posz, sem_pos_s, sem_pos_r, dz)
        wait_z(qx, sem_q_s, sem_q_r, dz)
        mixed, tops, sums = attend(dz)
        o_send[dz] = mixed.astype(bf16)
        st_send[dz] = jnp.concatenate(tops + sums, 0)
        o_copy(dz).start()
        st_copy(dz).start()
    for dz in (3, 2, 1):
        wait_z(o_recv, sem_o_s, sem_o_r, dz)
        wait_z(st_recv, sem_st_s, sem_st_r, dz)
        stats = st_recv[dz]
        partials.append(
            (o_recv[dz].astype(f32), [stats[0:1], stats[1:2]], [stats[2:3], stats[3:4]])
        )
    halves = []
    for head in range(2):
        top = functools.reduce(jnp.maximum, [tops[head] for _, tops, _ in partials])
        total, weight = 0.0, 0.0
        for mixed, tops, sums in partials:
            factor = jnp.exp(tops[head] - top)
            total = total + mixed[head * 64 : head * 64 + 64] * factor
            weight = weight + sums[head] * factor
        halves.append(total / weight)
    attention = jnp.concatenate(halves, 0).T.astype(bf16)
    for run in range(4):
        for half in range(2):
            att[half, run] = attention[run * 32 + half * 16 : run * 32 + half * 16 + 16]

    att_pair = remote(att.at[other], att_recv, sem_att_s, sem_att_r, partner_id)
    att_pair.start()
    wo_pair.wait_recv()
    att_pair.wait_recv()
    mine = jnp.concatenate([att[core].reshape(64, 128), att_recv[...].reshape(64, 128)], 1)
    product = jnp.dot(mine, wo[...].reshape(256, 2048), preferred_element_type=f32).reshape(4, 16, 2048)
    part[...] = product
    part_send[...] = product.astype(bf16)

    def part_copy(step):
        return remote(
            part_send.at[(zl + step) % 4], part_recv.at[step], sem_part_s.at[step], sem_part_r.at[step], run_id(step)
        )

    for step in (2, 1, 3):
        part_copy(step).start()
    summed = part[zl]
    for step in (1, 2, 3):
        part_copy(step).wait_recv()
    for step in (1, 2, 3):
        summed = summed + part_recv[step].astype(f32)
    out[0] = summed.astype(bf16)

    def drain(d, carry):
        for dz in range(4):
            id_plane(dz, d).wait_send()
            kv_copy(dz, d).wait_send()
        return carry

    lax.fori_loop(1, 16, drain, 0)
    for step in (1, 3):
        id_z(step).wait_send()
        pos_z(step).wait_send()
    id_relay.wait_send()
    pos_relay.wait_send()
    for step in (1, 2, 3):
        hid_run(step).wait_send()
        q_z(step).wait_send()
        o_copy(step).wait_send()
        st_copy(step).wait_send()
        part_copy(step).wait_send()
    for step in range(4):
        hid_pair(step).wait_send()
    wo_pair.wait_send()
    att_pair.wait_send()


def local(hidden, w_query, w_key, w_value, w_out, cache_keys, cache_values, stretch_count, stretch_ids, recompute_pos):
    half = np.arange(128) % 32
    freq = (ROPE_BASE ** (-(half * 2.0 / HEAD_DIM))).astype(np.float32)[None]
    vmem, smem, anywhere = (
        pl.BlockSpec(memory_space=pltpu.VMEM),
        pl.BlockSpec(memory_space=pltpu.SMEM),
        pl.BlockSpec(memory_space=pl.ANY),
    )
    f32, bf16, i32, dma = jnp.float32, jnp.bfloat16, jnp.int32, pltpu.SemaphoreType.DMA
    scratch = [
        pltpu.VMEM((8, 16, 2048), bf16),
        pltpu.VMEM((2048, 384), bf16),
        pltpu.VMEM((2, 128, 2048), bf16),
        pltpu.VMEM((256, 8, 128), f32),
        pltpu.VMEM((64, 1, 128), i32),
        pltpu.SMEM((64, 1, 128), i32),
        pltpu.VMEM((4, 1, 128), i32),
        pltpu.VMEM((4, 16, 96, 128), bf16),
        pltpu.VMEM((4, 16, 96, 128), bf16),
        pltpu.VMEM((4, 128, 128), bf16),
        pltpu.VMEM((2, 128, 128), bf16),
        pltpu.VMEM((48, 128), f32),
        pltpu.VMEM((48, 128), f32),
        pltpu.VMEM((16, 48, 128), i32),
        pltpu.VMEM((4, 128, 128), bf16),
        pltpu.VMEM((4, 128, 128), bf16),
        pltpu.VMEM((4, 4, 128), f32),
        pltpu.VMEM((4, 4, 128), f32),
        pltpu.VMEM((2, 4, 16, 128), bf16),
        pltpu.VMEM((4, 16, 128), bf16),
        pltpu.VMEM((4, 16, 2048), f32),
        pltpu.VMEM((4, 16, 2048), bf16),
        pltpu.VMEM((4, 16, 2048), bf16),
        dma((4,)),
        dma((4,)),
        dma((4,)),
        dma((4, 16)),
        dma((4, 16)),
        dma((4, 16)),
        dma((4,)),
        dma((4,)),
        dma((4,)),
        dma((4,)),
        dma((4, 16)),
        dma((4, 16)),
        dma((4,)),
        dma((4,)),
        dma((4,)),
        dma((4,)),
        dma((4,)),
        dma((4,)),
        dma((4,)),
        dma((4,)),
        dma,
        dma,
        dma,
        dma,
        dma((4,)),
        dma((4,)),
    ]
    return pl.pallas_call(
        kernel,
        out_shape=jax.ShapeDtypeStruct(hidden.shape, bf16),
        in_specs=[vmem, vmem, smem, vmem, vmem, vmem, vmem] + [anywhere] * 4,
        out_specs=vmem,
        scratch_shapes=scratch,
        compiler_params=pltpu.CompilerParams(
            collective_id=0, has_side_effects=True, vmem_limit_bytes=56 * 1024 * 1024
        ),
    )(
        hidden,
        stretch_ids,
        stretch_count,
        recompute_pos,
        jnp.asarray(freq),
        cache_keys,
        cache_values,
        w_query,
        w_key,
        w_value,
        w_out,
    )


def solution(mesh):
    placed = (
        P("group", "tp", None),
        P(None, "tp"),
        P(None, "tp"),
        P(None, "tp"),
        P("tp", None),
        P(None, "group", "tp"),
        P(None, "group", "tp"),
        P("group"),
        P("group", None),
        P("group", None),
    )
    return jax.shard_map(
        local, mesh=mesh, in_specs=placed, out_specs=P("group", "tp", None), check_vma=False
    )
```

```python
import functools

import jax
import jax.numpy as jnp
import numpy as np
from jax import lax
from jax.experimental import pallas as pl
from jax.experimental.pallas import tpu as pltpu
from jax.sharding import PartitionSpec as P

MESH = pl.DeviceIdType.MESH
HEAD_DIM = 64
STRETCH = 256
MAXCH = 12
ROPE_BASE = 130000.0
EPSILON = 1e-05
MASKED = -1e30
FLOOR = -1e29
FAR = 1 << 20
OFFSETS = (
    (0, 1), (0, 3), (1, 0), (3, 0),
    (1, 1), (1, 3), (3, 1), (3, 3), (0, 2), (2, 0),
    (1, 2), (2, 1), (3, 2), (2, 3), (2, 2),
)
STEP_X = sum(dx << (2 * i) for i, (dx, _) in enumerate(OFFSETS))
STEP_Y = sum(dy << (2 * i) for i, (_, dy) in enumerate(OFFSETS))
RINGS = ((0, 5), (5, 11), (11, 16))


def kernel(
    hidden_in,
    ids_in,
    count_in,
    pos_in,
    freq,
    keys_in,
    values_in,
    w_query,
    w_key,
    w_value,
    w_out,
    out,
    hidden,
    ids,
    count,
    pos,
    cache_keys,
    cache_values,
    normed,
    wqkv,
    wo,
    cache32,
    ids_s,
    posz,
    kv_send,
    kv,
    qx,
    fresh,
    key_cos,
    key_sin,
    key_pos,
    o_send,
    o_recv,
    st_send,
    st_recv,
    att,
    att_recv,
    part,
    part_send,
    part_recv,
    sem_load,
    sem_idz_s,
    sem_idz_r,
    sem_idp_s,
    sem_idp_r,
    sem_hid_s,
    sem_hid_r,
    sem_hidp_s,
    sem_hidp_r,
    sem_kv_s,
    sem_kv_r,
    sem_q_s,
    sem_q_r,
    sem_pos_s,
    sem_pos_r,
    sem_o_s,
    sem_o_r,
    sem_st_s,
    sem_st_r,
    sem_wo_s,
    sem_wo_r,
    sem_att_s,
    sem_att_r,
    sem_part_s,
    sem_part_r,
):
    f32, bf16 = jnp.float32, jnp.bfloat16
    g, t = lax.axis_index("group"), lax.axis_index("tp")
    gx, gz, gy = g // 16, (g // 4) % 4, g % 4
    s = gx * 4 + gy
    zl, core = t // 2, t % 2
    other = 1 - core

    def ahead(k):
        shift = 2 * (k - 1)
        return ((gx + (STEP_X >> shift) % 4) % 4) * 4 + (gy + (STEP_Y >> shift) % 4) % 4

    def behind(k):
        shift = 2 * (k - 1)
        return ((gx + 4 - (STEP_X >> shift) % 4) % 4) * 4 + (gy + 4 - (STEP_Y >> shift) % 4) % 4

    def plane_id(idx):
        return (((idx // 4) * 4 + gz) * 4 + idx % 4, t)

    def z_id(step):
        return ((gx * 4 + (gz + step) % 4) * 4 + gy, t)

    def run_id(step):
        return (g, ((zl + step) % 4) * 2 + core)

    partner_id = (g, zl * 2 + other)

    def remote(src, dst, send, recv, device):
        return pltpu.make_async_remote_copy(
            src_ref=src, dst_ref=dst, send_sem=send, recv_sem=recv, device_id=device, device_id_type=MESH
        )

    loads = [
        pltpu.make_async_copy(w_query, wqkv.at[:, 0:128], sem_load.at[0]),
        pltpu.make_async_copy(w_key, wqkv.at[:, 128:256], sem_load.at[1]),
        pltpu.make_async_copy(w_value, wqkv.at[:, 256:384], sem_load.at[2]),
        pltpu.make_async_copy(w_out, wo.at[0], sem_load.at[3]),
    ]
    small = [
        pltpu.make_async_copy(ids_in, ids, sem_load.at[4]),
        pltpu.make_async_copy(count_in, count, sem_load.at[5]),
        pltpu.make_async_copy(pos_in, pos, sem_load.at[6]),
        pltpu.make_async_copy(hidden_in.at[0], hidden, sem_load.at[7]),
        pltpu.make_async_copy(keys_in, cache_keys, sem_load.at[8]),
        pltpu.make_async_copy(values_in, cache_values, sem_load.at[9]),
    ]
    barrier = pltpu.get_barrier_semaphore()

    def greet(device):
        pl.semaphore_signal(barrier, inc=1, device_id=device, device_id_type=MESH)

    for step in (2, 1, 3):
        greet(z_id(step))

    def greet_plane(k, carry):
        greet(plane_id(ahead(k)))
        return carry

    lax.fori_loop(1, 16, greet_plane, 0)
    for step in (1, 2, 3):
        greet(run_id(step))
    greet(partner_id)

    for load in small + loads:
        load.start()
    for load in small[:3]:
        load.wait()
    for slot in range(MAXCH):
        ids_s[0, 0, slot] = ids[0, slot]
    ids_s[0, 0, MAXCH] = count[0]
    posz[0] = pos[...]
    small[3].wait()
    rows = hidden[...].astype(f32)
    normed[t] = (rows * lax.rsqrt(jnp.mean(rows * rows, axis=-1, keepdims=True) + EPSILON)).astype(bf16)

    def widen(i, carry):
        here = pl.ds(pl.multiple_of(i * 32, 32), 32)
        cache32[here, 0:4, :] = cache_keys[here].astype(f32)
        cache32[here, 4:8, :] = cache_values[here].astype(f32)
        return carry

    small[4].wait()
    small[5].wait()
    lax.fori_loop(0, 8, widen, 0)

    row48 = lax.broadcasted_iota(jnp.int32, (48, 128), 0)
    slot_angle = ((row48 // 4) * STRETCH).astype(f32) * freq[...]
    key_cos[...] = jnp.cos(slot_angle)
    key_sin[...] = jnp.sin(slot_angle)
    row48 = lax.broadcasted_iota(jnp.int32, (16, 48, 128), 1)
    place = lax.broadcasted_iota(jnp.int32, (16, 48, 128), 0)
    key_pos[...] = (row48 // 4) * STRETCH + 4 * (16 * (place // 4) + 4 * gz + place % 4) + row48 % 4

    pl.semaphore_wait(barrier, 22)

    def id_z(step):
        return remote(ids_s.at[0], ids_s.at[(4 - step) * 16], sem_idz_s.at[step], sem_idz_r.at[4 - step], z_id(step))

    def pos_z(step):
        return remote(posz.at[0], posz.at[4 - step], sem_pos_s.at[step], sem_pos_r.at[4 - step], z_id(step))

    def wait_z(ref, send, recv, dz):
        here = ref.at[dz]
        remote(here, here, send.at[dz], recv.at[dz], z_id(1)).wait_recv()

    def id_z_wait(dz):
        here = ids_s.at[dz * 16]
        remote(here, here, sem_idz_s.at[dz], sem_idz_r.at[dz], z_id(1)).wait_recv()

    def id_plane(dz, k):
        return remote(
            ids_s.at[dz * 16], ids_s.at[dz * 16 + k], sem_idp_s.at[dz, k], sem_idp_r.at[dz, k], plane_id(ahead(k))
        )

    def spread_ids(dz):
        def body(k, carry):
            id_plane(dz, k).start()
            return carry

        lax.fori_loop(1, 16, body, 0)

    for step in (2, 1, 3):
        id_z(step).start()
    spread_ids(0)

    def hid_run(step):
        here = normed.at[t]
        return remote(here, here, sem_hid_s.at[step], sem_hid_r.at[step], run_id(step))

    def hid_run_wait(step):
        here = normed.at[((zl + 4 - step) % 4) * 2 + core]
        remote(here, here, sem_hid_s.at[step], sem_hid_r.at[step], run_id(step)).wait_recv()

    def hid_pair(step):
        here = normed.at[((zl + 4 - step) % 4) * 2 + core]
        return remote(here, here, sem_hidp_s.at[step], sem_hidp_r.at[step], partner_id)

    def hid_pair_wait(step):
        here = normed.at[((zl + 4 - step) % 4) * 2 + other]
        remote(here, here, sem_hidp_s.at[step], sem_hidp_r.at[step], partner_id).wait_recv()

    for step in (2, 1, 3):
        hid_run(step).start()
    hid_pair(0).start()
    for step in (2, 1, 3):
        pos_z(step).start()
    loads[3].wait()
    wo_pair = remote(wo.at[0], wo.at[1], sem_wo_s, sem_wo_r, partner_id)
    wo_pair.start()

    low_rows = lax.broadcasted_iota(jnp.int32, (8, 128), 0) < 4

    def fill(row, target):
        for quad in range(3):
            key_rows, value_rows = [], []
            for pair in range(2):
                first = cache32[ids_s[row, 0, quad * 4 + pair * 2]]
                second = cache32[ids_s[row, 0, quad * 4 + pair * 2 + 1]]
                key_rows.append(jnp.where(low_rows, first, pltpu.roll(second, 4, 0)))
                value_rows.append(jnp.where(low_rows, pltpu.roll(first, 4, 0), second))
            target[quad * 16 : quad * 16 + 16, :] = jnp.concatenate(key_rows, 0).astype(bf16)
            target[48 + quad * 16 : 64 + quad * 16, :] = jnp.concatenate(value_rows, 0).astype(bf16)

    def kv_copy(dz, k):
        return remote(
            kv_send.at[dz, k], kv.at[dz, s], sem_kv_s.at[dz, k], sem_kv_r.at[dz, k], plane_id(behind(k))
        )

    def serve(dz, ring, backward=False):
        start, stop = ring

        def got(k, carry):
            id_plane(dz, k).wait_recv()
            return carry

        lax.fori_loop(max(start, 1), stop, got, 0)

        def send(i, carry):
            k = stop - 1 - i if backward else max(start, 1) + i
            fill(dz * 16 + k, kv_send.at[dz, k])
            kv_copy(dz, k).start()
            return carry

        lax.fori_loop(0, stop - max(start, 1), send, 0)
        if start == 0:
            fill(dz * 16, kv.at[dz, s])

    serve(0, RINGS[0])
    serve(0, RINGS[1])
    id_z_wait(1)
    spread_ids(1)
    id_z_wait(3)
    spread_ids(3)
    serve(0, RINGS[2])
    serve(1, RINGS[0])
    serve(3, RINGS[0])
    for step in (1, 2, 3):
        hid_run_wait(step)
        hid_pair(step).start()
    id_z_wait(2)
    spread_ids(2)
    serve(1, RINGS[1])
    serve(1, RINGS[2])

    posf = jnp.broadcast_to(pos[...].astype(f32), (128, 128)).T
    angle = posf * freq[...]
    cos_q, sin_q = jnp.cos(angle), jnp.sin(angle)
    lanes = lax.broadcasted_iota(jnp.int32, (128, 128), 1)
    lower = lanes % 64 < 32
    for load in loads[:3]:
        load.wait()
    for step in range(4):
        hid_pair_wait(step)

    def project(first, last):
        return jnp.dot(normed[...].reshape(128, 2048), wqkv[:, first:last], preferred_element_type=f32)

    def rotate(values):
        swapped = jnp.where(lower, -pltpu.roll(values, 96, 1), pltpu.roll(values, 32, 1))
        return (values * cos_q + swapped * sin_q).astype(bf16)

    qx[0] = (rotate(project(0, 128)).astype(f32) * HEAD_DIM**-0.5).astype(bf16)

    def q_z(step):
        return remote(qx.at[0], qx.at[4 - step], sem_q_s.at[step], sem_q_r.at[4 - step], z_id(step))

    for step in (2, 1, 3):
        q_z(step).start()
    serve(2, (0, 16), backward=True)
    serve(3, (5, 16), backward=True)
    projected = project(128, 384)
    fresh[0] = rotate(projected[:, 0:128])
    fresh[1] = projected[:, 128:256].astype(bf16)

    head0 = lanes < 64
    swap_row = lax.broadcasted_iota(jnp.int32, (128, 128), 0)
    swap = jnp.where(
        (lanes % 64 < 32) & (swap_row == lanes + 32),
        -1.0,
        jnp.where((lanes % 64 >= 32) & (swap_row == lanes - 32), 1.0, 0.0),
    ).astype(bf16)
    ones = jnp.ones((128, 128), bf16)
    last_dims = (((1,), (1,)), ((), ()))
    first_dims = (((0,), (0,)), ((), ()))

    def soften(keys, values, queries, usable):
        zero = jnp.zeros((), bf16)
        both = jnp.concatenate([jnp.where(head0, queries, zero), jnp.where(head0, zero, queries)], 0)
        scores = lax.dot_general(keys, both, last_dims, preferred_element_type=f32)
        tops, sums, weights = [], [], []
        for head in range(2):
            part_scores = jnp.where(usable, scores[:, head * 128 : head * 128 + 128], MASKED)
            top = jnp.maximum(jnp.max(part_scores, axis=0, keepdims=True), FLOOR)
            weight = jnp.exp(part_scores - top)
            tops.append(top)
            sums.append(jnp.sum(weight, axis=0, keepdims=True))
            weights.append(weight.astype(bf16))
        mixed = lax.dot_general(values, jnp.concatenate(weights, 1), first_dims, preferred_element_type=f32)
        return jnp.concatenate([mixed[0:64, 0:128], mixed[64:128, 128:256]], 0), tops, sums

    def attend(dz):
        def got(d, carry):
            here = kv.at[dz, ahead(d)]
            remote(here, here, sem_kv_s.at[dz, d], sem_kv_r.at[dz, d], plane_id(behind(d))).wait_recv()
            return carry

        lax.fori_loop(1, 16, got, 0)
        raw = kv[dz, :, 0:48, :]
        turned = jnp.dot(raw.reshape(768, 128), swap, preferred_element_type=f32).reshape(16, 48, 128)
        keys = (raw.astype(f32) * key_cos[...][None] + turned * key_sin[...][None]).astype(bf16).reshape(768, 128)
        values = kv[dz, :, 48:96, :].reshape(768, 128)
        place_of = key_pos[...].reshape(768, 128)
        pos_row = posz[dz]
        pos_col = jnp.broadcast_to(pos_row, (768, 128))
        same = jnp.where(place_of == pos_col, 1.0, 0.0).astype(bf16)
        marked = jnp.dot(same, ones, preferred_element_type=f32) > 0.5
        limit = ids_s[dz * 16, 0, MAXCH] * STRETCH
        usable = jnp.where(marked | (place_of >= limit), FAR, place_of) <= pos_col
        return soften(keys, values, qx[dz], usable)

    def o_copy(dz):
        return remote(o_send.at[dz], o_recv.at[4 - dz], sem_o_s.at[dz], sem_o_r.at[4 - dz], z_id(dz))

    def st_copy(dz):
        return remote(st_send.at[dz], st_recv.at[4 - dz], sem_st_s.at[dz], sem_st_r.at[4 - dz], z_id(dz))

    partials = [
        soften(fresh[0], fresh[1], qx[0], posf <= pos[...].astype(f32)),
        attend(0),
    ]
    for dz in (1, 2, 3):
        wait_z(posz, sem_pos_s, sem_pos_r, dz)
        wait_z(qx, sem_q_s, sem_q_r, dz)
        mixed, tops, sums = attend(dz)
        o_send[dz] = mixed.astype(bf16)
        st_send[dz] = jnp.concatenate(tops + sums, 0)
        o_copy(dz).start()
        st_copy(dz).start()
    for dz in (3, 2, 1):
        wait_z(o_recv, sem_o_s, sem_o_r, dz)
        wait_z(st_recv, sem_st_s, sem_st_r, dz)
        stats = st_recv[dz]
        partials.append(
            (o_recv[dz].astype(f32), [stats[0:1], stats[1:2]], [stats[2:3], stats[3:4]])
        )
    halves = []
    for head in range(2):
        top = functools.reduce(jnp.maximum, [tops[head] for _, tops, _ in partials])
        total, weight = 0.0, 0.0
        for mixed, tops, sums in partials:
            factor = jnp.exp(tops[head] - top)
            total = total + mixed[head * 64 : head * 64 + 64] * factor
            weight = weight + sums[head] * factor
        halves.append(total / weight)
    attention = jnp.concatenate(halves, 0).T.astype(bf16)
    for run in range(4):
        for half in range(2):
            att[half, run] = attention[run * 32 + half * 16 : run * 32 + half * 16 + 16]

    att_pair = remote(att.at[other], att_recv, sem_att_s, sem_att_r, partner_id)
    att_pair.start()
    wo_pair.wait_recv()
    att_pair.wait_recv()
    mine = jnp.concatenate([att[core].reshape(64, 128), att_recv[...].reshape(64, 128)], 1)
    product = jnp.dot(mine, wo[...].reshape(256, 2048), preferred_element_type=f32).reshape(4, 16, 2048)
    part[...] = product
    part_send[...] = product.astype(bf16)

    def part_copy(step):
        return remote(
            part_send.at[(zl + step) % 4], part_recv.at[step], sem_part_s.at[step], sem_part_r.at[step], run_id(step)
        )

    for step in (2, 1, 3):
        part_copy(step).start()
    summed = part[zl]
    for step in (1, 2, 3):
        part_copy(step).wait_recv()
    for step in (1, 2, 3):
        summed = summed + part_recv[step].astype(f32)
    out[0] = summed.astype(bf16)

    def drain(d, carry):
        for dz in range(4):
            id_plane(dz, d).wait_send()
            kv_copy(dz, d).wait_send()
        return carry

    lax.fori_loop(1, 16, drain, 0)
    for step in (1, 2, 3):
        id_z(step).wait_send()
        pos_z(step).wait_send()
        hid_run(step).wait_send()
        q_z(step).wait_send()
        o_copy(step).wait_send()
        st_copy(step).wait_send()
        part_copy(step).wait_send()
    for step in range(4):
        hid_pair(step).wait_send()
    wo_pair.wait_send()
    att_pair.wait_send()


def local(hidden, w_query, w_key, w_value, w_out, cache_keys, cache_values, stretch_count, stretch_ids, recompute_pos):
    half = np.arange(128) % 32
    freq = (ROPE_BASE ** (-(half * 2.0 / HEAD_DIM))).astype(np.float32)[None]
    vmem, anywhere = pl.BlockSpec(memory_space=pltpu.VMEM), pl.BlockSpec(memory_space=pl.ANY)
    f32, bf16, i32, dma = jnp.float32, jnp.bfloat16, jnp.int32, pltpu.SemaphoreType.DMA
    scratch = [
        pltpu.VMEM(hidden.shape[1:], bf16),
        pltpu.SMEM(stretch_ids.shape, i32),
        pltpu.SMEM(stretch_count.shape, i32),
        pltpu.VMEM(recompute_pos.shape, i32),
        pltpu.VMEM(cache_keys.shape, bf16),
        pltpu.VMEM(cache_values.shape, bf16),
        pltpu.VMEM((8, 16, 2048), bf16),
        pltpu.VMEM((2048, 384), bf16),
        pltpu.VMEM((2, 128, 2048), bf16),
        pltpu.VMEM((256, 8, 128), f32),
        pltpu.SMEM((64, 1, 128), i32),
        pltpu.VMEM((4, 1, 128), i32),
        pltpu.VMEM((4, 16, 96, 128), bf16),
        pltpu.VMEM((4, 16, 96, 128), bf16),
        pltpu.VMEM((4, 128, 128), bf16),
        pltpu.VMEM((2, 128, 128), bf16),
        pltpu.VMEM((48, 128), f32),
        pltpu.VMEM((48, 128), f32),
        pltpu.VMEM((16, 48, 128), i32),
        pltpu.VMEM((4, 128, 128), bf16),
        pltpu.VMEM((4, 128, 128), bf16),
        pltpu.VMEM((4, 4, 128), f32),
        pltpu.VMEM((4, 4, 128), f32),
        pltpu.VMEM((2, 4, 16, 128), bf16),
        pltpu.VMEM((4, 16, 128), bf16),
        pltpu.VMEM((4, 16, 2048), f32),
        pltpu.VMEM((4, 16, 2048), bf16),
        pltpu.VMEM((4, 16, 2048), bf16),
        dma((10,)),
        dma((4,)),
        dma((4,)),
        dma((4, 16)),
        dma((4, 16)),
        dma((4,)),
        dma((4,)),
        dma((4,)),
        dma((4,)),
        dma((4, 16)),
        dma((4, 16)),
        dma((4,)),
        dma((4,)),
        dma((4,)),
        dma((4,)),
        dma((4,)),
        dma((4,)),
        dma((4,)),
        dma((4,)),
        dma,
        dma,
        dma,
        dma,
        dma((4,)),
        dma((4,)),
    ]
    return pl.pallas_call(
        kernel,
        out_shape=jax.ShapeDtypeStruct(hidden.shape, bf16),
        in_specs=[anywhere] * 4 + [vmem] + [anywhere] * 6,
        out_specs=vmem,
        scratch_shapes=scratch,
        compiler_params=pltpu.CompilerParams(
            collective_id=0, has_side_effects=True, vmem_limit_bytes=56 * 1024 * 1024
        ),
    )(
        hidden,
        stretch_ids,
        stretch_count,
        recompute_pos,
        jnp.asarray(freq),
        cache_keys,
        cache_values,
        w_query,
        w_key,
        w_value,
        w_out,
    )


def solution(mesh):
    placed = (
        P("group", "tp", None),
        P(None, "tp"),
        P(None, "tp"),
        P(None, "tp"),
        P("tp", None),
        P(None, "group", "tp"),
        P(None, "group", "tp"),
        P("group"),
        P("group", None),
        P("group", None),
    )
    return jax.shard_map(
        local, mesh=mesh, in_specs=placed, out_specs=P("group", "tp", None), check_vma=False
    )
```

```python
import functools

import jax
import jax.numpy as jnp
import numpy as np
from jax import lax
from jax.experimental import pallas as pl
from jax.experimental.pallas import tpu as pltpu
from jax.sharding import PartitionSpec as P

MESH = pl.DeviceIdType.MESH
HEAD_DIM = 64
STRETCH = 256
MAXCH = 12
ROPE_BASE = 130000.0
EPSILON = 1e-05
MASKED = -1e30
FLOOR = -1e29
FAR = 1 << 20
OFFSETS = (
    (0, 1), (0, 3), (1, 0), (3, 0),
    (1, 1), (1, 3), (3, 1), (3, 3), (0, 2), (2, 0),
    (1, 2), (2, 1), (3, 2), (2, 3), (2, 2),
)
STEP_X = sum(dx << (2 * i) for i, (dx, _) in enumerate(OFFSETS))
STEP_Y = sum(dy << (2 * i) for i, (_, dy) in enumerate(OFFSETS))
RINGS = ((0, 5), (5, 11), (11, 16))


def kernel(
    hidden_in,
    ids_in,
    count_in,
    pos_in,
    freq,
    keys_in,
    values_in,
    w_query,
    w_key,
    w_value,
    w_out,
    out,
    hidden,
    ids,
    count,
    pos,
    cache_keys,
    cache_values,
    normed,
    wqkv,
    wo,
    cache32,
    ids_s,
    posz,
    kv_send,
    kv,
    qx,
    fresh,
    key_cos,
    key_sin,
    key_pos,
    o_send,
    o_recv,
    st_send,
    st_recv,
    share,
    part,
    part_send,
    part_recv,
    sem_load,
    sem_idz_s,
    sem_idz_r,
    sem_idp_s,
    sem_idp_r,
    sem_hid_s,
    sem_hid_r,
    sem_hidp_s,
    sem_hidp_r,
    sem_kv_s,
    sem_kv_r,
    sem_q_s,
    sem_q_r,
    sem_pos_s,
    sem_pos_r,
    sem_o_s,
    sem_o_r,
    sem_st_s,
    sem_st_r,
    sem_wo_s,
    sem_wo_r,
    sem_part_s,
    sem_part_r,
):
    f32, bf16 = jnp.float32, jnp.bfloat16
    g, t = lax.axis_index("group"), lax.axis_index("tp")
    gx, gz, gy = g // 16, (g // 4) % 4, g % 4
    s = gx * 4 + gy
    zl, core = t // 2, t % 2
    other = 1 - core

    def ahead(k):
        shift = 2 * (k - 1)
        return ((gx + (STEP_X >> shift) % 4) % 4) * 4 + (gy + (STEP_Y >> shift) % 4) % 4

    def behind(k):
        shift = 2 * (k - 1)
        return ((gx + 4 - (STEP_X >> shift) % 4) % 4) * 4 + (gy + 4 - (STEP_Y >> shift) % 4) % 4

    def plane_id(idx):
        return (((idx // 4) * 4 + gz) * 4 + idx % 4, t)

    def z_id(step):
        return ((gx * 4 + (gz + step) % 4) * 4 + gy, t)

    def z_half_id(step, half):
        return ((gx * 4 + (gz + step) % 4) * 4 + gy, zl * 2 + half)

    def run_id(step):
        return (g, ((zl + step) % 4) * 2 + core)

    partner_id = (g, zl * 2 + other)

    def remote(src, dst, send, recv, device):
        return pltpu.make_async_remote_copy(
            src_ref=src, dst_ref=dst, send_sem=send, recv_sem=recv, device_id=device, device_id_type=MESH
        )

    loads = [
        pltpu.make_async_copy(w_query, wqkv.at[:, 0:128], sem_load.at[0]),
        pltpu.make_async_copy(w_key, wqkv.at[:, 128:256], sem_load.at[1]),
        pltpu.make_async_copy(w_value, wqkv.at[:, 256:384], sem_load.at[2]),
        pltpu.make_async_copy(w_out, wo.at[core], sem_load.at[3]),
    ]
    small = [
        pltpu.make_async_copy(ids_in, ids, sem_load.at[4]),
        pltpu.make_async_copy(count_in, count, sem_load.at[5]),
        pltpu.make_async_copy(pos_in, pos, sem_load.at[6]),
        pltpu.make_async_copy(hidden_in.at[0], hidden, sem_load.at[7]),
        pltpu.make_async_copy(keys_in, cache_keys, sem_load.at[8]),
        pltpu.make_async_copy(values_in, cache_values, sem_load.at[9]),
    ]
    barrier = pltpu.get_barrier_semaphore()

    def greet(device):
        pl.semaphore_signal(barrier, inc=1, device_id=device, device_id_type=MESH)

    late = gz // 2

    @pl.when(late == 0)
    def _():
        greet(z_id(2))

    for step in (1, 3):
        greet(z_id(step))

    def greet_plane(k, carry):
        greet(plane_id(ahead(k)))
        return carry

    lax.fori_loop(1, 16, greet_plane, 0)
    for step in (1, 2, 3):
        greet(run_id(step))
    greet(partner_id)

    for load in small + loads:
        load.start()
    for load in small[:3]:
        load.wait()
    for slot in range(MAXCH):
        ids_s[0, 0, slot] = ids[0, slot]
    ids_s[0, 0, MAXCH] = count[0]
    posz[0] = pos[...]
    small[3].wait()
    rows = hidden[...].astype(f32)
    normed[t] = (rows * lax.rsqrt(jnp.mean(rows * rows, axis=-1, keepdims=True) + EPSILON)).astype(bf16)

    def widen(i, carry):
        here = pl.ds(pl.multiple_of(i * 32, 32), 32)
        cache32[here, 0:4, :] = cache_keys[here].astype(f32)
        cache32[here, 4:8, :] = cache_values[here].astype(f32)
        return carry

    small[4].wait()
    small[5].wait()
    lax.fori_loop(0, 8, widen, 0)

    row48 = lax.broadcasted_iota(jnp.int32, (48, 128), 0)
    slot_angle = ((row48 // 4) * STRETCH).astype(f32) * freq[...]
    key_cos[...] = jnp.cos(slot_angle)
    key_sin[...] = jnp.sin(slot_angle)
    row48 = lax.broadcasted_iota(jnp.int32, (16, 48, 128), 1)
    place = lax.broadcasted_iota(jnp.int32, (16, 48, 128), 0)
    key_pos[...] = (row48 // 4) * STRETCH + 4 * (16 * (place // 4) + 4 * gz + place % 4) + row48 % 4

    pl.semaphore_wait(barrier, 21 + late)

    def id_z(step):
        return remote(ids_s.at[0], ids_s.at[(4 - step) * 16], sem_idz_s.at[step], sem_idz_r.at[4 - step], z_id(step))

    def pos_z(step):
        return remote(posz.at[0], posz.at[4 - step], sem_pos_s.at[step], sem_pos_r.at[4 - step], z_id(step))

    def wait_z(ref, send, recv, dz):
        here = ref.at[dz]
        remote(here, here, send.at[dz], recv.at[dz], z_id(1)).wait_recv()

    def id_z_wait(dz):
        here = ids_s.at[dz * 16]
        remote(here, here, sem_idz_s.at[dz], sem_idz_r.at[dz], z_id(1)).wait_recv()

    def id_plane(dz, k):
        return remote(
            ids_s.at[dz * 16], ids_s.at[dz * 16 + k], sem_idp_s.at[dz, k], sem_idp_r.at[dz, k], plane_id(ahead(k))
        )

    def spread_ids(dz):
        def body(k, carry):
            id_plane(dz, k).start()
            return carry

        lax.fori_loop(1, 16, body, 0)

    id_relay = remote(ids_s.at[48], ids_s.at[32], sem_idz_s.at[0], sem_idz_r.at[2], z_id(1))
    pos_relay = remote(posz.at[3], posz.at[2], sem_pos_s.at[0], sem_pos_r.at[2], z_id(1))
    passing = (gz == 1) | (gz == 2)

    @pl.when(late == 1)
    def _():
        id_z(2).start()

    for step in (1, 3):
        id_z(step).start()
    spread_ids(0)

    def hid_run(step):
        here = normed.at[t]
        return remote(here, here, sem_hid_s.at[step], sem_hid_r.at[step], run_id(step))

    def hid_run_wait(step):
        here = normed.at[((zl + 4 - step) % 4) * 2 + core]
        remote(here, here, sem_hid_s.at[step], sem_hid_r.at[step], run_id(step)).wait_recv()

    def hid_pair(step):
        here = normed.at[((zl + 4 - step) % 4) * 2 + core]
        return remote(here, here, sem_hidp_s.at[step], sem_hidp_r.at[step], partner_id)

    def hid_pair_wait(step):
        here = normed.at[((zl + 4 - step) % 4) * 2 + other]
        remote(here, here, sem_hidp_s.at[step], sem_hidp_r.at[step], partner_id).wait_recv()

    for step in (2, 1, 3):
        hid_run(step).start()
    hid_pair(0).start()
    @pl.when(late == 1)
    def _():
        pos_z(2).start()

    for step in (1, 3):
        pos_z(step).start()
    loads[3].wait()
    wo_pair = remote(wo.at[core], wo.at[core], sem_wo_s, sem_wo_r, partner_id)
    wo_pair.start()

    low_rows = lax.broadcasted_iota(jnp.int32, (8, 128), 0) < 4

    def fill(row, target):
        for quad in range(3):
            key_rows, value_rows = [], []
            for pair in range(2):
                first = cache32[ids_s[row, 0, quad * 4 + pair * 2]]
                second = cache32[ids_s[row, 0, quad * 4 + pair * 2 + 1]]
                key_rows.append(jnp.where(low_rows, first, pltpu.roll(second, 4, 0)))
                value_rows.append(jnp.where(low_rows, pltpu.roll(first, 4, 0), second))
            target[quad * 16 : quad * 16 + 16, :] = jnp.concatenate(key_rows, 0).astype(bf16)
            target[48 + quad * 16 : 64 + quad * 16, :] = jnp.concatenate(value_rows, 0).astype(bf16)

    def kv_copy(dz, k):
        return remote(
            kv_send.at[dz, k], kv.at[dz, s], sem_kv_s.at[dz, k], sem_kv_r.at[dz, k], plane_id(behind(k))
        )

    def serve(dz, ring, backward=False):
        start, stop = ring

        def got(k, carry):
            id_plane(dz, k).wait_recv()
            return carry

        lax.fori_loop(max(start, 1), stop, got, 0)

        def send(i, carry):
            k = stop - 1 - i if backward else max(start, 1) + i
            fill(dz * 16 + k, kv_send.at[dz, k])
            kv_copy(dz, k).start()
            return carry

        lax.fori_loop(0, stop - max(start, 1), send, 0)
        if start == 0:
            fill(dz * 16, kv.at[dz, s])

    serve(0, RINGS[0])
    serve(0, RINGS[1])
    id_z_wait(3)

    @pl.when(passing)
    def _():
        id_relay.start()

    spread_ids(3)
    id_z_wait(1)
    spread_ids(1)
    wait_z(posz, sem_pos_s, sem_pos_r, 3)

    @pl.when(passing)
    def _():
        pos_relay.start()

    serve(0, RINGS[2])
    serve(1, RINGS[0])
    serve(3, RINGS[0])
    for step in (1, 2, 3):
        hid_run_wait(step)
        hid_pair(step).start()
    id_z_wait(2)
    spread_ids(2)
    serve(1, RINGS[1])
    serve(1, RINGS[2])

    posf = jnp.broadcast_to(pos[...].astype(f32), (128, 128)).T
    angle = posf * freq[...]
    cos_q, sin_q = jnp.cos(angle), jnp.sin(angle)
    lanes = lax.broadcasted_iota(jnp.int32, (128, 128), 1)
    lower = lanes % 64 < 32
    for load in loads[:3]:
        load.wait()
    for step in range(4):
        hid_pair_wait(step)

    def project(first, last):
        return jnp.dot(normed[...].reshape(128, 2048), wqkv[:, first:last], preferred_element_type=f32)

    def rotate(values):
        swapped = jnp.where(lower, -pltpu.roll(values, 96, 1), pltpu.roll(values, 32, 1))
        return (values * cos_q + swapped * sin_q).astype(bf16)

    qx[0] = (rotate(project(0, 128)).astype(f32) * HEAD_DIM**-0.5).astype(bf16)

    def q_z(step):
        return remote(qx.at[0], qx.at[4 - step], sem_q_s.at[step], sem_q_r.at[4 - step], z_id(step))

    for step in (2, 1, 3):
        q_z(step).start()
    serve(2, RINGS[0])
    serve(2, (5, 16), backward=True)
    serve(3, (5, 16), backward=True)
    projected = project(128, 384)
    fresh[0] = rotate(projected[:, 0:128])
    fresh[1] = projected[:, 128:256].astype(bf16)

    head0 = lanes < 64
    swap_row = lax.broadcasted_iota(jnp.int32, (128, 128), 0)
    swap = jnp.where(
        (lanes % 64 < 32) & (swap_row == lanes + 32),
        -1.0,
        jnp.where((lanes % 64 >= 32) & (swap_row == lanes - 32), 1.0, 0.0),
    ).astype(bf16)
    ones = jnp.ones((128, 128), bf16)
    last_dims = (((1,), (1,)), ((), ()))
    first_dims = (((0,), (0,)), ((), ()))

    def soften(keys, values, queries, usable):
        zero = jnp.zeros((), bf16)
        both = jnp.concatenate([jnp.where(head0, queries, zero), jnp.where(head0, zero, queries)], 0)
        scores = lax.dot_general(keys, both, last_dims, preferred_element_type=f32)
        tops, sums, weights = [], [], []
        for head in range(2):
            part_scores = jnp.where(usable, scores[:, head * 128 : head * 128 + 128], MASKED)
            top = jnp.maximum(jnp.max(part_scores, axis=0, keepdims=True), FLOOR)
            weight = jnp.exp(part_scores - top)
            tops.append(top)
            sums.append(jnp.sum(weight, axis=0, keepdims=True))
            weights.append(weight.astype(bf16))
        mixed = lax.dot_general(values, jnp.concatenate(weights, 1), first_dims, preferred_element_type=f32)
        return jnp.concatenate([mixed[0:64, 0:128], mixed[64:128, 128:256]], 0), tops, sums

    def attend(dz):
        def got(d, carry):
            here = kv.at[dz, ahead(d)]
            remote(here, here, sem_kv_s.at[dz, d], sem_kv_r.at[dz, d], plane_id(behind(d))).wait_recv()
            return carry

        lax.fori_loop(1, 16, got, 0)
        raw = kv[dz, :, 0:48, :]
        turned = jnp.dot(raw.reshape(768, 128), swap, preferred_element_type=f32).reshape(16, 48, 128)
        keys = (raw.astype(f32) * key_cos[...][None] + turned * key_sin[...][None]).astype(bf16).reshape(768, 128)
        values = kv[dz, :, 48:96, :].reshape(768, 128)
        place_of = key_pos[...].reshape(768, 128)
        pos_row = posz[dz]
        pos_col = jnp.broadcast_to(pos_row, (768, 128))
        same = jnp.where(place_of == pos_col, 1.0, 0.0).astype(bf16)
        marked = jnp.dot(same, ones, preferred_element_type=f32) > 0.5
        limit = ids_s[dz * 16, 0, MAXCH] * STRETCH
        usable = jnp.where(marked | (place_of >= limit), FAR, place_of) <= pos_col
        return soften(keys, values, qx[dz], usable)

    def o_copy(dz, half):
        device = z_half_id(dz, half)
        return remote(
            o_send.at[dz, half], o_recv.at[(4 - dz) % 4, core], sem_o_s.at[dz, half], sem_o_r.at[(4 - dz) % 4, core], device
        )

    def st_copy(dz, half):
        device = z_half_id(dz, half)
        return remote(
            st_send.at[dz], st_recv.at[(4 - dz) % 4, core], sem_st_s.at[dz, half], sem_st_r.at[(4 - dz) % 4, core], device
        )

    def back_wait(dz, half):
        here = o_recv.at[dz, half]
        remote(here, here, sem_o_s.at[dz, half], sem_o_r.at[dz, half], partner_id).wait_recv()
        here = st_recv.at[dz, half]
        remote(here, here, sem_st_s.at[dz, half], sem_st_r.at[dz, half], partner_id).wait_recv()

    def give(dz, mixed, tops, sums):
        turned = mixed.T.astype(bf16)
        for run in range(4):
            for half in range(2):
                o_send[dz, half, run] = turned[run * 32 + half * 16 : run * 32 + half * 16 + 16]
        st_send[dz] = jnp.concatenate(tops + sums, 0)
        o_copy(dz, other).start()
        st_copy(dz, other).start()
        if dz > 0:
            o_copy(dz, core).start()
            st_copy(dz, core).start()

    fresh_mixed, fresh_tops, fresh_sums = soften(fresh[0], fresh[1], qx[0], posf <= pos[...].astype(f32))
    own_mixed, own_tops, own_sums = attend(0)
    halves, tops, sums = [], [], []
    for head in range(2):
        top = jnp.maximum(fresh_tops[head], own_tops[head])
        fresh_factor, own_factor = jnp.exp(fresh_tops[head] - top), jnp.exp(own_tops[head] - top)
        here = slice(head * 64, head * 64 + 64)
        halves.append(fresh_mixed[here] * fresh_factor + own_mixed[here] * own_factor)
        tops.append(top)
        sums.append(fresh_sums[head] * fresh_factor + own_sums[head] * own_factor)
    give(0, jnp.concatenate(halves, 0), tops, sums)
    o_recv[0, core] = o_send[0, core]
    st_recv[0, core] = st_send[0]
    for dz in (1, 2, 3):
        if dz < 3:
            wait_z(posz, sem_pos_s, sem_pos_r, dz)
        wait_z(qx, sem_q_s, sem_q_r, dz)
        give(dz, *attend(dz))

    wo_pair.wait_recv()
    back_wait(0, other)
    for dz in (3, 2, 1):
        for half in range(2):
            back_wait(dz, half)
    stats = [[st_recv[dz, half] for half in range(2)] for dz in range(4)]
    tops = [jnp.concatenate([one[0:2] for one in pair], 0) for pair in stats]
    sums = [jnp.concatenate([one[2:4] for one in pair], 0) for pair in stats]
    top = functools.reduce(jnp.maximum, tops)
    factors = [jnp.exp(one - top) for one in tops]
    weight = functools.reduce(jnp.add, [factor * one for factor, one in zip(factors, sums)])
    shares = jnp.concatenate([factor / weight for factor in factors] + [jnp.zeros((112, 128), f32)], 0).T
    for run in range(4):
        for half in range(2):
            share[half, run] = shares[run * 32 + half * 16 : run * 32 + half * 16 + 16]
    own_share = share[core].reshape(64, 128)
    first_head = lax.broadcasted_iota(jnp.int32, (64, 128), 1) < 64
    sides = []
    for half in range(2):
        total = 0.0
        for dz in range(4):
            column = dz * 4 + half * 2
            factor = jnp.where(first_head, own_share[:, column : column + 1], own_share[:, column + 1 : column + 2])
            total = total + o_recv[dz, half].reshape(64, 128).astype(f32) * factor
        sides.append(total.astype(bf16))

    mine = jnp.concatenate(sides, 1)
    product = jnp.dot(mine, wo[...].reshape(256, 2048), preferred_element_type=f32).reshape(4, 16, 2048)
    part[...] = product
    part_send[...] = product.astype(bf16)

    def part_copy(step):
        return remote(
            part_send.at[(zl + step) % 4], part_recv.at[step], sem_part_s.at[step], sem_part_r.at[step], run_id(step)
        )

    for step in (2, 1, 3):
        part_copy(step).start()
    summed = part[zl]
    for step in (1, 2, 3):
        part_copy(step).wait_recv()
    for step in (1, 2, 3):
        summed = summed + part_recv[step].astype(f32)
    out[0] = summed.astype(bf16)

    def drain(d, carry):
        for dz in range(4):
            id_plane(dz, d).wait_send()
            kv_copy(dz, d).wait_send()
        return carry

    lax.fori_loop(1, 16, drain, 0)
    for step in (1, 3):
        id_z(step).wait_send()
        pos_z(step).wait_send()

    @pl.when(late == 1)
    def _():
        id_z(2).wait_send()
        pos_z(2).wait_send()

    @pl.when(passing)
    def _():
        id_relay.wait_send()
        pos_relay.wait_send()

    for step in (1, 2, 3):
        hid_run(step).wait_send()
        q_z(step).wait_send()
        for half in range(2):
            o_copy(step, half).wait_send()
            st_copy(step, half).wait_send()
        part_copy(step).wait_send()
    for step in range(4):
        hid_pair(step).wait_send()
    wo_pair.wait_send()
    o_copy(0, other).wait_send()
    st_copy(0, other).wait_send()


def local(hidden, w_query, w_key, w_value, w_out, cache_keys, cache_values, stretch_count, stretch_ids, recompute_pos):
    half = np.arange(128) % 32
    freq = (ROPE_BASE ** (-(half * 2.0 / HEAD_DIM))).astype(np.float32)[None]
    vmem, anywhere = pl.BlockSpec(memory_space=pltpu.VMEM), pl.BlockSpec(memory_space=pl.ANY)
    f32, bf16, i32, dma = jnp.float32, jnp.bfloat16, jnp.int32, pltpu.SemaphoreType.DMA
    scratch = [
        pltpu.VMEM(hidden.shape[1:], bf16),
        pltpu.SMEM(stretch_ids.shape, i32),
        pltpu.SMEM(stretch_count.shape, i32),
        pltpu.VMEM(recompute_pos.shape, i32),
        pltpu.VMEM(cache_keys.shape, bf16),
        pltpu.VMEM(cache_values.shape, bf16),
        pltpu.VMEM((8, 16, 2048), bf16),
        pltpu.VMEM((2048, 384), bf16),
        pltpu.VMEM((2, 128, 2048), bf16),
        pltpu.VMEM((256, 8, 128), f32),
        pltpu.SMEM((64, 1, 128), i32),
        pltpu.VMEM((4, 1, 128), i32),
        pltpu.VMEM((4, 16, 96, 128), bf16),
        pltpu.VMEM((4, 16, 96, 128), bf16),
        pltpu.VMEM((4, 128, 128), bf16),
        pltpu.VMEM((2, 128, 128), bf16),
        pltpu.VMEM((48, 128), f32),
        pltpu.VMEM((48, 128), f32),
        pltpu.VMEM((16, 48, 128), i32),
        pltpu.VMEM((4, 2, 4, 16, 128), bf16),
        pltpu.VMEM((4, 2, 4, 16, 128), bf16),
        pltpu.VMEM((4, 4, 128), f32),
        pltpu.VMEM((4, 2, 4, 128), f32),
        pltpu.VMEM((2, 4, 16, 128), f32),
        pltpu.VMEM((4, 16, 2048), f32),
        pltpu.VMEM((4, 16, 2048), bf16),
        pltpu.VMEM((4, 16, 2048), bf16),
        dma((10,)),
        dma((4,)),
        dma((4,)),
        dma((4, 16)),
        dma((4, 16)),
        dma((4,)),
        dma((4,)),
        dma((4,)),
        dma((4,)),
        dma((4, 16)),
        dma((4, 16)),
        dma((4,)),
        dma((4,)),
        dma((4,)),
        dma((4,)),
        dma((4, 2)),
        dma((4, 2)),
        dma((4, 2)),
        dma((4, 2)),
        dma,
        dma,
        dma((4,)),
        dma((4,)),
    ]
    return pl.pallas_call(
        kernel,
        out_shape=jax.ShapeDtypeStruct(hidden.shape, bf16),
        in_specs=[anywhere] * 4 + [vmem] + [anywhere] * 6,
        out_specs=vmem,
        scratch_shapes=scratch,
        compiler_params=pltpu.CompilerParams(
            collective_id=0, has_side_effects=True, vmem_limit_bytes=56 * 1024 * 1024
        ),
    )(
        hidden,
        stretch_ids,
        stretch_count,
        recompute_pos,
        jnp.asarray(freq),
        cache_keys,
        cache_values,
        w_query,
        w_key,
        w_value,
        w_out,
    )


def solution(mesh):
    placed = (
        P("group", "tp", None),
        P(None, "tp"),
        P(None, "tp"),
        P(None, "tp"),
        P("tp", None),
        P(None, "group", "tp"),
        P(None, "group", "tp"),
        P("group"),
        P("group", None),
        P("group", None),
    )
    return jax.shard_map(
        local, mesh=mesh, in_specs=placed, out_specs=P("group", "tp", None), check_vma=False
    )
```

```python
import functools

import jax
import jax.numpy as jnp
import numpy as np
from jax import lax
from jax.experimental import pallas as pl
from jax.experimental.pallas import tpu as pltpu
from jax.sharding import PartitionSpec as P

MESH = pl.DeviceIdType.MESH
HEAD_DIM = 64
STRETCH = 256
MAXCH = 12
ROPE_BASE = 130000.0
EPSILON = 1e-05
MASKED = -1e30
FLOOR = -1e29
FAR = 1 << 20
OFFSETS = (
    (0, 1), (0, 3), (1, 0), (3, 0),
    (1, 1), (1, 3), (3, 1), (3, 3), (0, 2), (2, 0),
    (1, 2), (2, 1), (3, 2), (2, 3), (2, 2),
)
STEP_X = sum(dx << (2 * i) for i, (dx, _) in enumerate(OFFSETS))
STEP_Y = sum(dy << (2 * i) for i, (_, dy) in enumerate(OFFSETS))
RINGS = ((0, 5), (5, 11), (11, 16))


def kernel(
    hidden_in,
    ids_in,
    count_in,
    pos_in,
    freq,
    keys_in,
    values_in,
    w_query,
    w_key,
    w_value,
    w_out,
    out,
    hidden,
    ids,
    count,
    pos,
    cache_keys,
    cache_values,
    normed,
    wqkv,
    wo,
    cache32,
    ids_s,
    posz,
    kv_send,
    kv,
    qx,
    fresh,
    key_cos,
    key_sin,
    key_pos,
    pos_down,
    query_cos,
    query_sin,
    o_send,
    o_recv,
    st_send,
    st_recv,
    share,
    part,
    part_send,
    part_recv,
    sem_load,
    sem_idz_s,
    sem_idz_r,
    sem_idp_s,
    sem_idp_r,
    sem_hid_s,
    sem_hid_r,
    sem_hidp_s,
    sem_hidp_r,
    sem_kv_s,
    sem_kv_r,
    sem_q_s,
    sem_q_r,
    sem_pos_s,
    sem_pos_r,
    sem_o_s,
    sem_o_r,
    sem_st_s,
    sem_st_r,
    sem_wo_s,
    sem_wo_r,
    sem_part_s,
    sem_part_r,
):
    f32, bf16 = jnp.float32, jnp.bfloat16
    g, t = lax.axis_index("group"), lax.axis_index("tp")
    gx, gz, gy = g // 16, (g // 4) % 4, g % 4
    s = gx * 4 + gy
    zl, core = t // 2, t % 2
    other = 1 - core

    def ahead(k):
        shift = 2 * (k - 1)
        return ((gx + (STEP_X >> shift) % 4) % 4) * 4 + (gy + (STEP_Y >> shift) % 4) % 4

    def behind(k):
        shift = 2 * (k - 1)
        return ((gx + 4 - (STEP_X >> shift) % 4) % 4) * 4 + (gy + 4 - (STEP_Y >> shift) % 4) % 4

    def plane_id(idx):
        return (((idx // 4) * 4 + gz) * 4 + idx % 4, t)

    def z_id(step):
        return ((gx * 4 + (gz + step) % 4) * 4 + gy, t)

    def z_half_id(step, half):
        return ((gx * 4 + (gz + step) % 4) * 4 + gy, zl * 2 + half)

    def run_id(step):
        return (g, ((zl + step) % 4) * 2 + core)

    partner_id = (g, zl * 2 + other)

    def remote(src, dst, send, recv, device):
        return pltpu.make_async_remote_copy(
            src_ref=src, dst_ref=dst, send_sem=send, recv_sem=recv, device_id=device, device_id_type=MESH
        )

    loads = [
        pltpu.make_async_copy(w_query, wqkv.at[:, 0:128], sem_load.at[0]),
        pltpu.make_async_copy(w_key, wqkv.at[:, 128:256], sem_load.at[1]),
        pltpu.make_async_copy(w_value, wqkv.at[:, 256:384], sem_load.at[2]),
        pltpu.make_async_copy(w_out, wo.at[core], sem_load.at[3]),
    ]
    small = [
        pltpu.make_async_copy(ids_in, ids, sem_load.at[4]),
        pltpu.make_async_copy(count_in, count, sem_load.at[5]),
        pltpu.make_async_copy(pos_in, pos, sem_load.at[6]),
        pltpu.make_async_copy(hidden_in.at[0], hidden, sem_load.at[7]),
        pltpu.make_async_copy(keys_in, cache_keys, sem_load.at[8]),
        pltpu.make_async_copy(values_in, cache_values, sem_load.at[9]),
    ]
    barrier = pltpu.get_barrier_semaphore()

    def greet(device):
        pl.semaphore_signal(barrier, inc=1, device_id=device, device_id_type=MESH)

    late = gz // 2

    @pl.when(late == 0)
    def _():
        greet(z_id(2))

    for step in (1, 3):
        greet(z_id(step))

    def greet_plane(k, carry):
        greet(plane_id(ahead(k)))
        return carry

    lax.fori_loop(1, 16, greet_plane, 0)
    for step in (1, 2, 3):
        greet(run_id(step))
    greet(partner_id)

    for load in small + loads:
        load.start()
    for load in small[:3]:
        load.wait()
    for slot in range(MAXCH):
        ids_s[0, 0, slot] = ids[0, slot]
    ids_s[0, 0, MAXCH] = count[0]
    posz[0] = pos[...]
    small[3].wait()
    rows = hidden[...].astype(f32)
    normed[t] = (rows * lax.rsqrt(jnp.mean(rows * rows, axis=-1, keepdims=True) + EPSILON)).astype(bf16)

    def widen(i, carry):
        here = pl.ds(pl.multiple_of(i * 32, 32), 32)
        cache32[here, 0:4, :] = cache_keys[here].astype(f32)
        cache32[here, 4:8, :] = cache_values[here].astype(f32)
        return carry

    small[4].wait()
    small[5].wait()
    lax.fori_loop(0, 8, widen, 0)

    row48 = lax.broadcasted_iota(jnp.int32, (48, 128), 0)
    slot_angle = ((row48 // 4) * STRETCH).astype(f32) * freq[...]
    key_cos[...] = jnp.cos(slot_angle)
    key_sin[...] = jnp.sin(slot_angle)
    row48 = lax.broadcasted_iota(jnp.int32, (16, 48, 128), 1)
    place = lax.broadcasted_iota(jnp.int32, (16, 48, 128), 0)
    key_pos[...] = (row48 // 4) * STRETCH + 4 * (16 * (place // 4) + 4 * gz + place % 4) + row48 % 4

    pos_down[...] = jnp.broadcast_to(pos[...].astype(f32), (128, 128)).T
    angle = pos_down[...] * freq[...]
    query_cos[...] = jnp.cos(angle)
    query_sin[...] = jnp.sin(angle)

    pl.semaphore_wait(barrier, 21 + late)

    def id_z(step):
        return remote(ids_s.at[0], ids_s.at[(4 - step) * 16], sem_idz_s.at[step], sem_idz_r.at[4 - step], z_id(step))

    def pos_z(step):
        return remote(posz.at[0], posz.at[4 - step], sem_pos_s.at[step], sem_pos_r.at[4 - step], z_id(step))

    def wait_z(ref, send, recv, dz):
        here = ref.at[dz]
        remote(here, here, send.at[dz], recv.at[dz], z_id(1)).wait_recv()

    def id_z_wait(dz):
        here = ids_s.at[dz * 16]
        remote(here, here, sem_idz_s.at[dz], sem_idz_r.at[dz], z_id(1)).wait_recv()

    def id_plane(dz, k):
        return remote(
            ids_s.at[dz * 16], ids_s.at[dz * 16 + k], sem_idp_s.at[dz, k], sem_idp_r.at[dz, k], plane_id(ahead(k))
        )

    def spread_ids(dz):
        def body(k, carry):
            id_plane(dz, k).start()
            return carry

        lax.fori_loop(1, 16, body, 0)

    id_relay = remote(ids_s.at[48], ids_s.at[32], sem_idz_s.at[0], sem_idz_r.at[2], z_id(1))
    pos_relay = remote(posz.at[3], posz.at[2], sem_pos_s.at[0], sem_pos_r.at[2], z_id(1))
    passing = (gz == 1) | (gz == 2)

    @pl.when(late == 1)
    def _():
        id_z(2).start()

    for step in (1, 3):
        id_z(step).start()
    spread_ids(0)

    def hid_run(step):
        here = normed.at[t]
        return remote(here, here, sem_hid_s.at[step], sem_hid_r.at[step], run_id(step))

    def hid_run_wait(step):
        here = normed.at[((zl + 4 - step) % 4) * 2 + core]
        remote(here, here, sem_hid_s.at[step], sem_hid_r.at[step], run_id(step)).wait_recv()

    def hid_pair(step):
        here = normed.at[((zl + 4 - step) % 4) * 2 + core]
        return remote(here, here, sem_hidp_s.at[step], sem_hidp_r.at[step], partner_id)

    def hid_pair_wait(step):
        here = normed.at[((zl + 4 - step) % 4) * 2 + other]
        remote(here, here, sem_hidp_s.at[step], sem_hidp_r.at[step], partner_id).wait_recv()

    for step in (2, 1, 3):
        hid_run(step).start()
    hid_pair(0).start()
    @pl.when(late == 1)
    def _():
        pos_z(2).start()

    for step in (1, 3):
        pos_z(step).start()
    wo_pair = remote(wo.at[core], wo.at[core], sem_wo_s, sem_wo_r, partner_id)

    low_rows = lax.broadcasted_iota(jnp.int32, (8, 128), 0) < 4

    def fill(row, target):
        for quad in range(3):
            key_rows, value_rows = [], []
            for pair in range(2):
                first = cache32[ids_s[row, 0, quad * 4 + pair * 2]]
                second = cache32[ids_s[row, 0, quad * 4 + pair * 2 + 1]]
                key_rows.append(jnp.where(low_rows, first, pltpu.roll(second, 4, 0)))
                value_rows.append(jnp.where(low_rows, pltpu.roll(first, 4, 0), second))
            target[quad * 16 : quad * 16 + 16, :] = jnp.concatenate(key_rows, 0).astype(bf16)
            target[48 + quad * 16 : 64 + quad * 16, :] = jnp.concatenate(value_rows, 0).astype(bf16)

    def kv_copy(dz, k):
        return remote(
            kv_send.at[dz, k], kv.at[dz, s], sem_kv_s.at[dz, k], sem_kv_r.at[dz, k], plane_id(behind(k))
        )

    def serve(dz, ring, backward=False):
        start, stop = ring

        def got(k, carry):
            id_plane(dz, k).wait_recv()
            return carry

        lax.fori_loop(max(start, 1), stop, got, 0)

        def send(i, carry):
            k = stop - 1 - i if backward else max(start, 1) + i
            fill(dz * 16 + k, kv_send.at[dz, k])
            kv_copy(dz, k).start()
            return carry

        lax.fori_loop(0, stop - max(start, 1), send, 0)
        if start == 0:
            fill(dz * 16, kv.at[dz, s])

    serve(0, RINGS[0])
    serve(0, RINGS[1])
    id_z_wait(3)

    @pl.when(passing)
    def _():
        id_relay.start()

    spread_ids(3)
    id_z_wait(1)
    spread_ids(1)
    wait_z(posz, sem_pos_s, sem_pos_r, 3)

    @pl.when(passing)
    def _():
        pos_relay.start()

    serve(0, RINGS[2])
    serve(1, RINGS[0])
    for step in (1, 2, 3):
        hid_run_wait(step)
        hid_pair(step).start()
    id_z_wait(2)
    spread_ids(2)
    serve(1, RINGS[1])
    serve(1, RINGS[2])

    lanes = lax.broadcasted_iota(jnp.int32, (128, 128), 1)
    lower = lanes % 64 < 32
    for load in loads[:3]:
        load.wait()
    for step in range(4):
        hid_pair_wait(step)

    def project(first, last):
        return jnp.dot(normed[...].reshape(128, 2048), wqkv[:, first:last], preferred_element_type=f32)

    def rotate(values):
        swapped = jnp.where(lower, -pltpu.roll(values, 96, 1), pltpu.roll(values, 32, 1))
        return (values * query_cos[...] + swapped * query_sin[...]).astype(bf16)

    qx[0] = (rotate(project(0, 128)).astype(f32) * HEAD_DIM**-0.5).astype(bf16)

    def q_z(step):
        return remote(qx.at[0], qx.at[4 - step], sem_q_s.at[step], sem_q_r.at[4 - step], z_id(step))

    for step in (2, 1, 3):
        q_z(step).start()
    loads[3].wait()
    wo_pair.start()
    serve(2, RINGS[0])
    serve(2, (5, 16), backward=True)
    serve(3, (0, 16), backward=True)
    projected = project(128, 384)
    fresh[0] = rotate(projected[:, 0:128])
    fresh[1] = projected[:, 128:256].astype(bf16)

    head0 = lanes < 64
    swap_row = lax.broadcasted_iota(jnp.int32, (128, 128), 0)
    swap = jnp.where(
        (lanes % 64 < 32) & (swap_row == lanes + 32),
        -1.0,
        jnp.where((lanes % 64 >= 32) & (swap_row == lanes - 32), 1.0, 0.0),
    ).astype(bf16)
    ones = jnp.ones((128, 128), bf16)
    last_dims = (((1,), (1,)), ((), ()))
    first_dims = (((0,), (0,)), ((), ()))

    def soften(keys, values, queries, usable):
        zero = jnp.zeros((), bf16)
        both = jnp.concatenate([jnp.where(head0, queries, zero), jnp.where(head0, zero, queries)], 0)
        scores = lax.dot_general(keys, both, last_dims, preferred_element_type=f32)
        tops, sums, weights = [], [], []
        for head in range(2):
            part_scores = jnp.where(usable, scores[:, head * 128 : head * 128 + 128], MASKED)
            top = jnp.maximum(jnp.max(part_scores, axis=0, keepdims=True), FLOOR)
            weight = jnp.exp(part_scores - top)
            tops.append(top)
            sums.append(jnp.sum(weight, axis=0, keepdims=True))
            weights.append(weight.astype(bf16))
        mixed = lax.dot_general(values, jnp.concatenate(weights, 1), first_dims, preferred_element_type=f32)
        return jnp.concatenate([mixed[0:64, 0:128], mixed[64:128, 128:256]], 0), tops, sums

    def visible(dz):
        place_of = key_pos[...].reshape(768, 128)
        pos_col = jnp.broadcast_to(posz[dz], (768, 128))
        same = jnp.where(place_of == pos_col, 1.0, 0.0).astype(bf16)
        marked = jnp.dot(same, ones, preferred_element_type=f32) > 0.5
        limit = ids_s[dz * 16, 0, MAXCH] * STRETCH
        return jnp.where(marked | (place_of >= limit), FAR, place_of) <= pos_col

    def attend(dz):
        usable = visible(dz)
        if dz > 0:
            wait_z(qx, sem_q_s, sem_q_r, dz)

        def got(d, carry):
            here = kv.at[dz, ahead(d)]
            remote(here, here, sem_kv_s.at[dz, d], sem_kv_r.at[dz, d], plane_id(behind(d))).wait_recv()
            return carry

        lax.fori_loop(1, 16, got, 0)
        raw = kv[dz, :, 0:48, :]
        turned = jnp.dot(raw.reshape(768, 128), swap, preferred_element_type=f32).reshape(16, 48, 128)
        keys = (raw.astype(f32) * key_cos[...][None] + turned * key_sin[...][None]).astype(bf16).reshape(768, 128)
        values = kv[dz, :, 48:96, :].reshape(768, 128)
        return soften(keys, values, qx[dz], usable)

    def o_copy(dz, half):
        device = z_half_id(dz, half)
        return remote(
            o_send.at[dz, half], o_recv.at[(4 - dz) % 4, core], sem_o_s.at[dz, half], sem_o_r.at[(4 - dz) % 4, core], device
        )

    def st_copy(dz, half):
        device = z_half_id(dz, half)
        return remote(
            st_send.at[dz], st_recv.at[(4 - dz) % 4, core], sem_st_s.at[dz, half], sem_st_r.at[(4 - dz) % 4, core], device
        )

    def back_wait(dz, half):
        here = o_recv.at[dz, half]
        remote(here, here, sem_o_s.at[dz, half], sem_o_r.at[dz, half], partner_id).wait_recv()
        here = st_recv.at[dz, half]
        remote(here, here, sem_st_s.at[dz, half], sem_st_r.at[dz, half], partner_id).wait_recv()

    def give(dz, mixed, tops, sums):
        turned = mixed.T.astype(bf16)
        for run in range(4):
            for half in range(2):
                o_send[dz, half, run] = turned[run * 32 + half * 16 : run * 32 + half * 16 + 16]
        st_send[dz] = jnp.concatenate(tops + sums, 0)
        o_copy(dz, other).start()
        st_copy(dz, other).start()
        if dz > 0:
            o_copy(dz, core).start()
            st_copy(dz, core).start()

    fresh_mixed, fresh_tops, fresh_sums = soften(fresh[0], fresh[1], qx[0], pos_down[...] <= pos[...].astype(f32))
    own_mixed, own_tops, own_sums = attend(0)
    halves, tops, sums = [], [], []
    for head in range(2):
        top = jnp.maximum(fresh_tops[head], own_tops[head])
        fresh_factor, own_factor = jnp.exp(fresh_tops[head] - top), jnp.exp(own_tops[head] - top)
        here = slice(head * 64, head * 64 + 64)
        halves.append(fresh_mixed[here] * fresh_factor + own_mixed[here] * own_factor)
        tops.append(top)
        sums.append(fresh_sums[head] * fresh_factor + own_sums[head] * own_factor)
    give(0, jnp.concatenate(halves, 0), tops, sums)
    o_recv[0, core] = o_send[0, core]
    st_recv[0, core] = st_send[0]
    for dz in (1, 2, 3):
        if dz < 3:
            wait_z(posz, sem_pos_s, sem_pos_r, dz)
        give(dz, *attend(dz))

    wo_pair.wait_recv()
    back_wait(0, other)
    for dz in (3, 2, 1):
        for half in range(2):
            back_wait(dz, half)
    stats = [[st_recv[dz, half] for half in range(2)] for dz in range(4)]
    tops = [jnp.concatenate([one[0:2] for one in pair], 0) for pair in stats]
    sums = [jnp.concatenate([one[2:4] for one in pair], 0) for pair in stats]
    top = functools.reduce(jnp.maximum, tops)
    factors = [jnp.exp(one - top) for one in tops]
    weight = functools.reduce(jnp.add, [factor * one for factor, one in zip(factors, sums)])
    shares = jnp.concatenate([factor / weight for factor in factors] + [jnp.zeros((112, 128), f32)], 0).T
    for run in range(4):
        for half in range(2):
            share[half, run] = shares[run * 32 + half * 16 : run * 32 + half * 16 + 16]
    own_share = share[core].reshape(64, 128)
    first_head = lax.broadcasted_iota(jnp.int32, (64, 128), 1) < 64
    sides = []
    for half in range(2):
        total = 0.0
        for dz in range(4):
            column = dz * 4 + half * 2
            factor = jnp.where(first_head, own_share[:, column : column + 1], own_share[:, column + 1 : column + 2])
            total = total + o_recv[dz, half].reshape(64, 128).astype(f32) * factor
        sides.append(total.astype(bf16))

    mine = jnp.concatenate(sides, 1)
    product = jnp.dot(mine, wo[...].reshape(256, 2048), preferred_element_type=f32).reshape(4, 16, 2048)
    part[...] = product
    part_send[...] = product.astype(bf16)

    def part_copy(step):
        return remote(
            part_send.at[(zl + step) % 4], part_recv.at[step], sem_part_s.at[step], sem_part_r.at[step], run_id(step)
        )

    for step in (2, 1, 3):
        part_copy(step).start()
    summed = part[zl]
    for step in (1, 2, 3):
        part_copy(step).wait_recv()
    for step in (1, 2, 3):
        summed = summed + part_recv[step].astype(f32)
    out[0] = summed.astype(bf16)

    def drain(d, carry):
        for dz in range(4):
            id_plane(dz, d).wait_send()
            kv_copy(dz, d).wait_send()
        return carry

    lax.fori_loop(1, 16, drain, 0)
    for step in (1, 3):
        id_z(step).wait_send()
        pos_z(step).wait_send()

    @pl.when(late == 1)
    def _():
        id_z(2).wait_send()
        pos_z(2).wait_send()

    @pl.when(passing)
    def _():
        id_relay.wait_send()
        pos_relay.wait_send()

    for step in (1, 2, 3):
        hid_run(step).wait_send()
        q_z(step).wait_send()
        for half in range(2):
            o_copy(step, half).wait_send()
            st_copy(step, half).wait_send()
        part_copy(step).wait_send()
    for step in range(4):
        hid_pair(step).wait_send()
    wo_pair.wait_send()
    o_copy(0, other).wait_send()
    st_copy(0, other).wait_send()


def local(hidden, w_query, w_key, w_value, w_out, cache_keys, cache_values, stretch_count, stretch_ids, recompute_pos):
    half = np.arange(128) % 32
    freq = (ROPE_BASE ** (-(half * 2.0 / HEAD_DIM))).astype(np.float32)[None]
    vmem, anywhere = pl.BlockSpec(memory_space=pltpu.VMEM), pl.BlockSpec(memory_space=pl.ANY)
    f32, bf16, i32, dma = jnp.float32, jnp.bfloat16, jnp.int32, pltpu.SemaphoreType.DMA
    scratch = [
        pltpu.VMEM(hidden.shape[1:], bf16),
        pltpu.SMEM(stretch_ids.shape, i32),
        pltpu.SMEM(stretch_count.shape, i32),
        pltpu.VMEM(recompute_pos.shape, i32),
        pltpu.VMEM(cache_keys.shape, bf16),
        pltpu.VMEM(cache_values.shape, bf16),
        pltpu.VMEM((8, 16, 2048), bf16),
        pltpu.VMEM((2048, 384), bf16),
        pltpu.VMEM((2, 128, 2048), bf16),
        pltpu.VMEM((256, 8, 128), f32),
        pltpu.SMEM((64, 1, 128), i32),
        pltpu.VMEM((4, 1, 128), i32),
        pltpu.VMEM((4, 16, 96, 128), bf16),
        pltpu.VMEM((4, 16, 96, 128), bf16),
        pltpu.VMEM((4, 128, 128), bf16),
        pltpu.VMEM((2, 128, 128), bf16),
        pltpu.VMEM((48, 128), f32),
        pltpu.VMEM((48, 128), f32),
        pltpu.VMEM((16, 48, 128), i32),
        pltpu.VMEM((128, 128), f32),
        pltpu.VMEM((128, 128), f32),
        pltpu.VMEM((128, 128), f32),
        pltpu.VMEM((4, 2, 4, 16, 128), bf16),
        pltpu.VMEM((4, 2, 4, 16, 128), bf16),
        pltpu.VMEM((4, 4, 128), f32),
        pltpu.VMEM((4, 2, 4, 128), f32),
        pltpu.VMEM((2, 4, 16, 128), f32),
        pltpu.VMEM((4, 16, 2048), f32),
        pltpu.VMEM((4, 16, 2048), bf16),
        pltpu.VMEM((4, 16, 2048), bf16),
        dma((10,)),
        dma((4,)),
        dma((4,)),
        dma((4, 16)),
        dma((4, 16)),
        dma((4,)),
        dma((4,)),
        dma((4,)),
        dma((4,)),
        dma((4, 16)),
        dma((4, 16)),
        dma((4,)),
        dma((4,)),
        dma((4,)),
        dma((4,)),
        dma((4, 2)),
        dma((4, 2)),
        dma((4, 2)),
        dma((4, 2)),
        dma,
        dma,
        dma((4,)),
        dma((4,)),
    ]
    return pl.pallas_call(
        kernel,
        out_shape=jax.ShapeDtypeStruct(hidden.shape, bf16),
        in_specs=[anywhere] * 4 + [vmem] + [anywhere] * 6,
        out_specs=vmem,
        scratch_shapes=scratch,
        compiler_params=pltpu.CompilerParams(
            collective_id=0, has_side_effects=True, vmem_limit_bytes=56 * 1024 * 1024
        ),
    )(
        hidden,
        stretch_ids,
        stretch_count,
        recompute_pos,
        jnp.asarray(freq),
        cache_keys,
        cache_values,
        w_query,
        w_key,
        w_value,
        w_out,
    )


def solution(mesh):
    placed = (
        P("group", "tp", None),
        P(None, "tp"),
        P(None, "tp"),
        P(None, "tp"),
        P("tp", None),
        P(None, "group", "tp"),
        P(None, "group", "tp"),
        P("group"),
        P("group", None),
        P("group", None),
    )
    return jax.shard_map(
        local, mesh=mesh, in_specs=placed, out_specs=P("group", "tp", None), check_vma=False
    )
```

```python
import functools

import jax
import jax.numpy as jnp
import numpy as np
from jax import lax
from jax.experimental import pallas as pl
from jax.experimental.pallas import tpu as pltpu
from jax.sharding import PartitionSpec as P

MESH = pl.DeviceIdType.MESH
HEAD_DIM = 64
STRETCH = 256
MAXCH = 12
ROPE_BASE = 130000.0
EPSILON = 1e-05
MASKED = -1e30
FLOOR = -1e29
FAR = 1 << 20
OFFSETS = (
    (0, 1), (0, 3), (1, 0), (3, 0),
    (1, 1), (1, 3), (3, 1), (3, 3), (0, 2), (2, 0),
    (1, 2), (2, 1), (3, 2), (2, 3), (2, 2),
)
STEP_X = sum(dx << (2 * i) for i, (dx, _) in enumerate(OFFSETS))
STEP_Y = sum(dy << (2 * i) for i, (_, dy) in enumerate(OFFSETS))
RINGS = ((0, 5), (5, 11), (11, 16))


def kernel(
    hidden_in,
    ids_in,
    count_in,
    pos_in,
    freq,
    keys_in,
    values_in,
    w_query,
    w_key,
    w_value,
    w_out,
    out,
    hidden,
    ids,
    count,
    pos,
    cache_keys,
    cache_values,
    normed,
    wqkv,
    wo,
    cache32,
    ids_s,
    posz,
    kv_send,
    kv,
    qx,
    fresh,
    key_cos,
    key_sin,
    key_pos,
    pos_down,
    query_cos,
    query_sin,
    o_send,
    o_recv,
    st_send,
    st_recv,
    share,
    part,
    part_send,
    part_recv,
    sem_load,
    sem_idz_s,
    sem_idz_r,
    sem_idp_s,
    sem_idp_r,
    sem_hid_s,
    sem_hid_r,
    sem_hidp_s,
    sem_hidp_r,
    sem_kv_s,
    sem_kv_r,
    sem_q_s,
    sem_q_r,
    sem_pos_s,
    sem_pos_r,
    sem_o_s,
    sem_o_r,
    sem_st_s,
    sem_st_r,
    sem_wo_s,
    sem_wo_r,
    sem_part_s,
    sem_part_r,
):
    f32, bf16 = jnp.float32, jnp.bfloat16
    g, t = lax.axis_index("group"), lax.axis_index("tp")
    gx, gz, gy = g // 16, (g // 4) % 4, g % 4
    s = gx * 4 + gy
    zl, core = t // 2, t % 2
    other = 1 - core

    def ahead(k):
        shift = 2 * (k - 1)
        return ((gx + (STEP_X >> shift) % 4) % 4) * 4 + (gy + (STEP_Y >> shift) % 4) % 4

    def behind(k):
        shift = 2 * (k - 1)
        return ((gx + 4 - (STEP_X >> shift) % 4) % 4) * 4 + (gy + 4 - (STEP_Y >> shift) % 4) % 4

    def plane_id(idx):
        return (((idx // 4) * 4 + gz) * 4 + idx % 4, t)

    def z_id(step):
        return ((gx * 4 + (gz + step) % 4) * 4 + gy, t)

    def z_half_id(step, half):
        return ((gx * 4 + (gz + step) % 4) * 4 + gy, zl * 2 + half)

    def run_id(step):
        return (g, ((zl + step) % 4) * 2 + core)

    partner_id = (g, zl * 2 + other)
    crossing_first = (2, 3 - 2 * (zl % 2), 1 + 2 * (zl % 2))

    def remote(src, dst, send, recv, device):
        return pltpu.make_async_remote_copy(
            src_ref=src, dst_ref=dst, send_sem=send, recv_sem=recv, device_id=device, device_id_type=MESH
        )

    loads = [
        pltpu.make_async_copy(w_query, wqkv.at[:, 0:128], sem_load.at[0]),
        pltpu.make_async_copy(w_key, wqkv.at[:, 128:256], sem_load.at[1]),
        pltpu.make_async_copy(w_value, wqkv.at[:, 256:384], sem_load.at[2]),
        pltpu.make_async_copy(w_out, wo.at[core], sem_load.at[3]),
    ]
    small = [
        pltpu.make_async_copy(ids_in, ids, sem_load.at[4]),
        pltpu.make_async_copy(count_in, count, sem_load.at[5]),
        pltpu.make_async_copy(pos_in, pos, sem_load.at[6]),
        pltpu.make_async_copy(hidden_in.at[0], hidden, sem_load.at[7]),
        pltpu.make_async_copy(keys_in, cache_keys, sem_load.at[8]),
        pltpu.make_async_copy(values_in, cache_values, sem_load.at[9]),
    ]
    barrier = pltpu.get_barrier_semaphore()

    def greet(device):
        pl.semaphore_signal(barrier, inc=1, device_id=device, device_id_type=MESH)

    late = gz // 2

    @pl.when(late == 0)
    def _():
        greet(z_id(2))

    for step in (1, 3):
        greet(z_id(step))

    def greet_plane(k, carry):
        greet(plane_id(ahead(k)))
        return carry

    lax.fori_loop(1, 16, greet_plane, 0)
    for step in (1, 2, 3):
        greet(run_id(step))
    greet(partner_id)

    for load in small + loads:
        load.start()
    for load in small[:3]:
        load.wait()
    for slot in range(MAXCH):
        ids_s[0, 0, slot] = ids[0, slot]
    ids_s[0, 0, MAXCH] = count[0]
    posz[0] = pos[...]
    small[3].wait()
    rows = hidden[...].astype(f32)
    normed[t] = (rows * lax.rsqrt(jnp.mean(rows * rows, axis=-1, keepdims=True) + EPSILON)).astype(bf16)

    def widen(i, carry):
        here = pl.ds(pl.multiple_of(i * 32, 32), 32)
        cache32[here, 0:4, :] = cache_keys[here].astype(f32)
        cache32[here, 4:8, :] = cache_values[here].astype(f32)
        return carry

    small[4].wait()
    small[5].wait()
    lax.fori_loop(0, 8, widen, 0)

    row48 = lax.broadcasted_iota(jnp.int32, (48, 128), 0)
    slot_angle = ((row48 // 4) * STRETCH).astype(f32) * freq[...]
    key_cos[...] = jnp.cos(slot_angle)
    key_sin[...] = jnp.sin(slot_angle)
    row48 = lax.broadcasted_iota(jnp.int32, (16, 48, 128), 1)
    place = lax.broadcasted_iota(jnp.int32, (16, 48, 128), 0)
    key_pos[...] = (row48 // 4) * STRETCH + 4 * (16 * (place // 4) + 4 * gz + place % 4) + row48 % 4

    pos_down[...] = jnp.broadcast_to(pos[...].astype(f32), (128, 128)).T
    angle = pos_down[...] * freq[...]
    query_cos[...] = jnp.cos(angle)
    query_sin[...] = jnp.sin(angle)

    pl.semaphore_wait(barrier, 21 + late)

    def id_z(step):
        return remote(ids_s.at[0], ids_s.at[(4 - step) * 16], sem_idz_s.at[step], sem_idz_r.at[4 - step], z_id(step))

    def pos_z(step):
        return remote(posz.at[0], posz.at[4 - step], sem_pos_s.at[step], sem_pos_r.at[4 - step], z_id(step))

    def wait_z(ref, send, recv, dz):
        here = ref.at[dz]
        remote(here, here, send.at[dz], recv.at[dz], z_id(1)).wait_recv()

    def id_z_wait(dz):
        here = ids_s.at[dz * 16]
        remote(here, here, sem_idz_s.at[dz], sem_idz_r.at[dz], z_id(1)).wait_recv()

    def id_plane(dz, k):
        return remote(
            ids_s.at[dz * 16], ids_s.at[dz * 16 + k], sem_idp_s.at[dz, k], sem_idp_r.at[dz, k], plane_id(ahead(k))
        )

    def spread_ids(dz):
        def body(k, carry):
            id_plane(dz, k).start()
            return carry

        lax.fori_loop(1, 16, body, 0)

    id_relay = remote(ids_s.at[48], ids_s.at[32], sem_idz_s.at[0], sem_idz_r.at[2], z_id(1))
    pos_relay = remote(posz.at[3], posz.at[2], sem_pos_s.at[0], sem_pos_r.at[2], z_id(1))
    passing = (gz == 1) | (gz == 2)

    @pl.when(late == 1)
    def _():
        id_z(2).start()

    for step in (1, 3):
        id_z(step).start()
    spread_ids(0)

    def hid_run(step):
        here = normed.at[t]
        return remote(here, here, sem_hid_s.at[step], sem_hid_r.at[step], run_id(step))

    def hid_run_wait(step):
        here = normed.at[((zl + 4 - step) % 4) * 2 + core]
        remote(here, here, sem_hid_s.at[step], sem_hid_r.at[step], run_id(step)).wait_recv()

    def hid_pair(step):
        here = normed.at[((zl + 4 - step) % 4) * 2 + core]
        return remote(here, here, sem_hidp_s.at[step], sem_hidp_r.at[step], partner_id)

    def hid_pair_wait(step):
        here = normed.at[((zl + 4 - step) % 4) * 2 + other]
        remote(here, here, sem_hidp_s.at[step], sem_hidp_r.at[step], partner_id).wait_recv()

    for step in crossing_first:
        hid_run(step).start()
    hid_pair(0).start()
    @pl.when(late == 1)
    def _():
        pos_z(2).start()

    for step in (1, 3):
        pos_z(step).start()
    wo_pair = remote(wo.at[core], wo.at[core], sem_wo_s, sem_wo_r, partner_id)

    low_rows = lax.broadcasted_iota(jnp.int32, (8, 128), 0) < 4

    def fill(row, target):
        for quad in range(3):
            key_rows, value_rows = [], []
            for pair in range(2):
                first = cache32[ids_s[row, 0, quad * 4 + pair * 2]]
                second = cache32[ids_s[row, 0, quad * 4 + pair * 2 + 1]]
                key_rows.append(jnp.where(low_rows, first, pltpu.roll(second, 4, 0)))
                value_rows.append(jnp.where(low_rows, pltpu.roll(first, 4, 0), second))
            target[quad * 16 : quad * 16 + 16, :] = jnp.concatenate(key_rows, 0).astype(bf16)
            target[48 + quad * 16 : 64 + quad * 16, :] = jnp.concatenate(value_rows, 0).astype(bf16)

    def kv_copy(dz, k):
        return remote(
            kv_send.at[dz, k], kv.at[dz, s], sem_kv_s.at[dz, k], sem_kv_r.at[dz, k], plane_id(behind(k))
        )

    def serve(dz, ring, backward=False):
        start, stop = ring

        def got(k, carry):
            id_plane(dz, k).wait_recv()
            return carry

        lax.fori_loop(max(start, 1), stop, got, 0)

        def send(i, carry):
            k = stop - 1 - i if backward else max(start, 1) + i
            fill(dz * 16 + k, kv_send.at[dz, k])
            kv_copy(dz, k).start()
            return carry

        lax.fori_loop(0, stop - max(start, 1), send, 0)
        if start == 0:
            fill(dz * 16, kv.at[dz, s])

    serve(0, RINGS[0])
    serve(0, RINGS[1])
    id_z_wait(3)

    @pl.when(passing)
    def _():
        id_relay.start()

    spread_ids(3)
    id_z_wait(1)
    spread_ids(1)
    wait_z(posz, sem_pos_s, sem_pos_r, 3)

    @pl.when(passing)
    def _():
        pos_relay.start()

    serve(0, RINGS[2])
    serve(1, RINGS[0])
    for step in (1, 2, 3):
        hid_run_wait(step)
        hid_pair(step).start()
    id_z_wait(2)
    spread_ids(2)
    serve(1, RINGS[1])
    serve(1, RINGS[2])

    lanes = lax.broadcasted_iota(jnp.int32, (128, 128), 1)
    lower = lanes % 64 < 32
    for load in loads[:3]:
        load.wait()
    for step in range(4):
        hid_pair_wait(step)

    def project(first, last):
        return jnp.dot(normed[...].reshape(128, 2048), wqkv[:, first:last], preferred_element_type=f32)

    def rotate(values):
        swapped = jnp.where(lower, -pltpu.roll(values, 96, 1), pltpu.roll(values, 32, 1))
        return (values * query_cos[...] + swapped * query_sin[...]).astype(bf16)

    qx[0] = (rotate(project(0, 128)).astype(f32) * HEAD_DIM**-0.5).astype(bf16)

    def q_z(step):
        return remote(qx.at[0], qx.at[4 - step], sem_q_s.at[step], sem_q_r.at[4 - step], z_id(step))

    for step in (2, 1, 3):
        q_z(step).start()
    loads[3].wait()
    wo_pair.start()
    serve(2, RINGS[0])
    serve(2, (5, 16), backward=True)
    serve(3, (0, 16), backward=True)
    projected = project(128, 384)
    fresh[0] = rotate(projected[:, 0:128])
    fresh[1] = projected[:, 128:256].astype(bf16)

    head0 = lanes < 64
    swap_row = lax.broadcasted_iota(jnp.int32, (128, 128), 0)
    swap = jnp.where(
        (lanes % 64 < 32) & (swap_row == lanes + 32),
        -1.0,
        jnp.where((lanes % 64 >= 32) & (swap_row == lanes - 32), 1.0, 0.0),
    ).astype(bf16)
    ones = jnp.ones((128, 128), bf16)
    last_dims = (((1,), (1,)), ((), ()))
    first_dims = (((0,), (0,)), ((), ()))

    def soften(keys, values, queries, usable):
        zero = jnp.zeros((), bf16)
        both = jnp.concatenate([jnp.where(head0, queries, zero), jnp.where(head0, zero, queries)], 0)
        scores = lax.dot_general(keys, both, last_dims, preferred_element_type=f32)
        tops, sums, weights = [], [], []
        for head in range(2):
            part_scores = jnp.where(usable, scores[:, head * 128 : head * 128 + 128], MASKED)
            top = jnp.maximum(jnp.max(part_scores, axis=0, keepdims=True), FLOOR)
            weight = jnp.exp(part_scores - top)
            tops.append(top)
            sums.append(jnp.sum(weight, axis=0, keepdims=True))
            weights.append(weight.astype(bf16))
        mixed = lax.dot_general(values, jnp.concatenate(weights, 1), first_dims, preferred_element_type=f32)
        return jnp.concatenate([mixed[0:64, 0:128], mixed[64:128, 128:256]], 0), tops, sums

    def visible(dz):
        place_of = key_pos[...].reshape(768, 128)
        pos_col = jnp.broadcast_to(posz[dz], (768, 128))
        same = jnp.where(place_of == pos_col, 1.0, 0.0).astype(bf16)
        marked = jnp.dot(same, ones, preferred_element_type=f32) > 0.5
        limit = ids_s[dz * 16, 0, MAXCH] * STRETCH
        return jnp.where(marked | (place_of >= limit), FAR, place_of) <= pos_col

    def attend(dz):
        usable = visible(dz)
        if dz > 0:
            wait_z(qx, sem_q_s, sem_q_r, dz)

        def got(d, carry):
            here = kv.at[dz, ahead(d)]
            remote(here, here, sem_kv_s.at[dz, d], sem_kv_r.at[dz, d], plane_id(behind(d))).wait_recv()
            return carry

        lax.fori_loop(1, 16, got, 0)
        raw = kv[dz, :, 0:48, :]
        turned = jnp.dot(raw.reshape(768, 128), swap, preferred_element_type=f32).reshape(16, 48, 128)
        keys = (raw.astype(f32) * key_cos[...][None] + turned * key_sin[...][None]).astype(bf16).reshape(768, 128)
        values = kv[dz, :, 48:96, :].reshape(768, 128)
        return soften(keys, values, qx[dz], usable)

    def o_copy(dz, half):
        device = z_half_id(dz, half)
        return remote(
            o_send.at[dz, half], o_recv.at[(4 - dz) % 4, core], sem_o_s.at[dz, half], sem_o_r.at[(4 - dz) % 4, core], device
        )

    def st_copy(dz, half):
        device = z_half_id(dz, half)
        return remote(
            st_send.at[dz], st_recv.at[(4 - dz) % 4, core], sem_st_s.at[dz, half], sem_st_r.at[(4 - dz) % 4, core], device
        )

    def back_wait(dz, half):
        here = o_recv.at[dz, half]
        remote(here, here, sem_o_s.at[dz, half], sem_o_r.at[dz, half], partner_id).wait_recv()
        here = st_recv.at[dz, half]
        remote(here, here, sem_st_s.at[dz, half], sem_st_r.at[dz, half], partner_id).wait_recv()

    def give(dz, mixed, tops, sums):
        turned = mixed.T.astype(bf16)
        for run in range(4):
            for half in range(2):
                o_send[dz, half, run] = turned[run * 32 + half * 16 : run * 32 + half * 16 + 16]
        st_send[dz] = jnp.concatenate(tops + sums, 0)
        o_copy(dz, other).start()
        st_copy(dz, other).start()
        if dz > 0:
            o_copy(dz, core).start()
            st_copy(dz, core).start()

    fresh_mixed, fresh_tops, fresh_sums = soften(fresh[0], fresh[1], qx[0], pos_down[...] <= pos[...].astype(f32))
    own_mixed, own_tops, own_sums = attend(0)
    halves, tops, sums = [], [], []
    for head in range(2):
        top = jnp.maximum(fresh_tops[head], own_tops[head])
        fresh_factor, own_factor = jnp.exp(fresh_tops[head] - top), jnp.exp(own_tops[head] - top)
        here = slice(head * 64, head * 64 + 64)
        halves.append(fresh_mixed[here] * fresh_factor + own_mixed[here] * own_factor)
        tops.append(top)
        sums.append(fresh_sums[head] * fresh_factor + own_sums[head] * own_factor)
    give(0, jnp.concatenate(halves, 0), tops, sums)
    o_recv[0, core] = o_send[0, core]
    st_recv[0, core] = st_send[0]
    for dz in (1, 2, 3):
        if dz < 3:
            wait_z(posz, sem_pos_s, sem_pos_r, dz)
        give(dz, *attend(dz))

    wo_pair.wait_recv()
    back_wait(0, other)
    for dz in (3, 2, 1):
        for half in range(2):
            back_wait(dz, half)
    stats = [[st_recv[dz, half] for half in range(2)] for dz in range(4)]
    tops = [jnp.concatenate([one[0:2] for one in pair], 0) for pair in stats]
    sums = [jnp.concatenate([one[2:4] for one in pair], 0) for pair in stats]
    top = functools.reduce(jnp.maximum, tops)
    factors = [jnp.exp(one - top) for one in tops]
    weight = functools.reduce(jnp.add, [factor * one for factor, one in zip(factors, sums)])
    shares = jnp.concatenate([factor / weight for factor in factors] + [jnp.zeros((112, 128), f32)], 0).T
    for run in range(4):
        for half in range(2):
            share[half, run] = shares[run * 32 + half * 16 : run * 32 + half * 16 + 16]
    own_share = share[core].reshape(64, 128)
    first_head = lax.broadcasted_iota(jnp.int32, (64, 128), 1) < 64
    sides = []
    for half in range(2):
        total = 0.0
        for dz in range(4):
            column = dz * 4 + half * 2
            factor = jnp.where(first_head, own_share[:, column : column + 1], own_share[:, column + 1 : column + 2])
            total = total + o_recv[dz, half].reshape(64, 128).astype(f32) * factor
        sides.append(total.astype(bf16))

    mine = jnp.concatenate(sides, 1)
    product = jnp.dot(mine, wo[...].reshape(256, 2048), preferred_element_type=f32).reshape(4, 16, 2048)
    part[...] = product
    part_send[...] = product.astype(bf16)

    def part_copy(step):
        return remote(
            part_send.at[(zl + step) % 4], part_recv.at[step], sem_part_s.at[step], sem_part_r.at[step], run_id(step)
        )

    for step in crossing_first:
        part_copy(step).start()
    summed = part[zl]
    for step in (1, 2, 3):
        part_copy(step).wait_recv()
    for step in (1, 2, 3):
        summed = summed + part_recv[step].astype(f32)
    out[0] = summed.astype(bf16)

    def drain(d, carry):
        for dz in range(4):
            id_plane(dz, d).wait_send()
            kv_copy(dz, d).wait_send()
        return carry

    lax.fori_loop(1, 16, drain, 0)
    for step in (1, 3):
        id_z(step).wait_send()
        pos_z(step).wait_send()

    @pl.when(late == 1)
    def _():
        id_z(2).wait_send()
        pos_z(2).wait_send()

    @pl.when(passing)
    def _():
        id_relay.wait_send()
        pos_relay.wait_send()

    for step in (1, 2, 3):
        hid_run(step).wait_send()
        q_z(step).wait_send()
        for half in range(2):
            o_copy(step, half).wait_send()
            st_copy(step, half).wait_send()
        part_copy(step).wait_send()
    for step in range(4):
        hid_pair(step).wait_send()
    wo_pair.wait_send()
    o_copy(0, other).wait_send()
    st_copy(0, other).wait_send()


def local(hidden, w_query, w_key, w_value, w_out, cache_keys, cache_values, stretch_count, stretch_ids, recompute_pos):
    half = np.arange(128) % 32
    freq = (ROPE_BASE ** (-(half * 2.0 / HEAD_DIM))).astype(np.float32)[None]
    vmem, anywhere = pl.BlockSpec(memory_space=pltpu.VMEM), pl.BlockSpec(memory_space=pl.ANY)
    f32, bf16, i32, dma = jnp.float32, jnp.bfloat16, jnp.int32, pltpu.SemaphoreType.DMA
    scratch = [
        pltpu.VMEM(hidden.shape[1:], bf16),
        pltpu.SMEM(stretch_ids.shape, i32),
        pltpu.SMEM(stretch_count.shape, i32),
        pltpu.VMEM(recompute_pos.shape, i32),
        pltpu.VMEM(cache_keys.shape, bf16),
        pltpu.VMEM(cache_values.shape, bf16),
        pltpu.VMEM((8, 16, 2048), bf16),
        pltpu.VMEM((2048, 384), bf16),
        pltpu.VMEM((2, 128, 2048), bf16),
        pltpu.VMEM((256, 8, 128), f32),
        pltpu.SMEM((64, 1, 128), i32),
        pltpu.VMEM((4, 1, 128), i32),
        pltpu.VMEM((4, 16, 96, 128), bf16),
        pltpu.VMEM((4, 16, 96, 128), bf16),
        pltpu.VMEM((4, 128, 128), bf16),
        pltpu.VMEM((2, 128, 128), bf16),
        pltpu.VMEM((48, 128), f32),
        pltpu.VMEM((48, 128), f32),
        pltpu.VMEM((16, 48, 128), i32),
        pltpu.VMEM((128, 128), f32),
        pltpu.VMEM((128, 128), f32),
        pltpu.VMEM((128, 128), f32),
        pltpu.VMEM((4, 2, 4, 16, 128), bf16),
        pltpu.VMEM((4, 2, 4, 16, 128), bf16),
        pltpu.VMEM((4, 4, 128), f32),
        pltpu.VMEM((4, 2, 4, 128), f32),
        pltpu.VMEM((2, 4, 16, 128), f32),
        pltpu.VMEM((4, 16, 2048), f32),
        pltpu.VMEM((4, 16, 2048), bf16),
        pltpu.VMEM((4, 16, 2048), bf16),
        dma((10,)),
        dma((4,)),
        dma((4,)),
        dma((4, 16)),
        dma((4, 16)),
        dma((4,)),
        dma((4,)),
        dma((4,)),
        dma((4,)),
        dma((4, 16)),
        dma((4, 16)),
        dma((4,)),
        dma((4,)),
        dma((4,)),
        dma((4,)),
        dma((4, 2)),
        dma((4, 2)),
        dma((4, 2)),
        dma((4, 2)),
        dma,
        dma,
        dma((4,)),
        dma((4,)),
    ]
    return pl.pallas_call(
        kernel,
        out_shape=jax.ShapeDtypeStruct(hidden.shape, bf16),
        in_specs=[anywhere] * 4 + [vmem] + [anywhere] * 6,
        out_specs=vmem,
        scratch_shapes=scratch,
        compiler_params=pltpu.CompilerParams(
            collective_id=0, has_side_effects=True, vmem_limit_bytes=56 * 1024 * 1024
        ),
    )(
        hidden,
        stretch_ids,
        stretch_count,
        recompute_pos,
        jnp.asarray(freq),
        cache_keys,
        cache_values,
        w_query,
        w_key,
        w_value,
        w_out,
    )


def solution(mesh):
    placed = (
        P("group", "tp", None),
        P(None, "tp"),
        P(None, "tp"),
        P(None, "tp"),
        P("tp", None),
        P(None, "group", "tp"),
        P(None, "group", "tp"),
        P("group"),
        P("group", None),
        P("group", None),
    )
    return jax.shard_map(
        local, mesh=mesh, in_specs=placed, out_specs=P("group", "tp", None), check_vma=False
    )
```
